32 devices in a mesh: dp: 4 (over x, core), mp: 8 (over z, y).
Axes of the slice: x: 2, y: 2, z: 4, core: 2. Of those that a mesh axis runs over, the one named last changes fastest.
Arguments:
- tokens: bfloat16 [16384, 1792], P(('dp', 'mp')), may hold values from -12 to 12
- first_norm_gain: float32 [1792], replicated, may hold values from 0.25 to 1.75
- query_weight: bfloat16 [1792, 896], replicated, may hold values from -0.144098955 to 0.144098955
- key_weight: bfloat16 [1792, 896], replicated, may hold values from -3.5670397 to 3.5670397
- value_weight: bfloat16 [1792, 896], replicated, may hold values from -0.125 to 0.125
- output_weight: bfloat16 [896, 1792], replicated, may hold values from -0.1875 to 0.1875
- lengths: int32 [256], P(('dp', 'mp')), may hold values from 1 to 64, as said below
- request_adapter: int32 [256], P(('dp', 'mp')), may hold values from 0 to 31, as said below
- slot_adapter_ids: int32 [32], replicated, may hold values from 0 to 31, as said below
- plugin_shrink_maps: bfloat16 [32, 1792, 32], P('mp'), may hold values from -0.125 to 0.125
- plugin_grow_maps: bfloat16 [32, 2, 16, 896], P('mp'), may hold values from -1.5 to 1.5
- device_token_order: int32 [32, 512], P(('dp', 'mp')), may hold values from 0 to 511, each once within a row
- second_norm_gain: float32 [1792], replicated, may hold values from 0.25 to 1.75
- gate_weight: bfloat16 [1792, 3584], P(('dp', 'mp')), may hold values from -0.125 to 0.125
- up_weight: bfloat16 [1792, 3584], P(('dp', 'mp')), may hold values from -0.125 to 0.125
Outputs:
- residual: bfloat16 [16384, 1792], P(('dp', 'mp'))
- hidden: bfloat16 [16384, 3584], P(('dp', 'mp'))
The draws below stay inside these ranges and needn't reach their ends.
Inputs may be any that keep to these rules, and one draw needn't show every extreme that they name: `slot_adapter_ids`: a permutation of the adapter ids; slot s lives on index s // 4 of mp. `request_adapter`: the 8 requests of one device use adapters whose slots lie on distinct indices of mp. `lengths`: on every device some request has length 64.
All inputs are finite; a program needn't handle non-finite values.
Results may differ from the reference program's by a relative error of at most 0.011.
Values may be sent and summed in bfloat16 or wider, within the bound.
A program may use at most 192 MiB of HBM per device.

```python
import jax
import jax.numpy as jnp
from jax import lax

EMBED_SPAN = 1792
HEADS = 8
HD = 112
FF = 3584
LATENT_BREADTH = 16
APD = 4
REQ_DEV = 8
SLOTR = 64
WINDOW = 32
SINKS = 4
ATTN_CHANNELS = 896
TOK_DEV = 512
REQUESTS = 256
TOKENS = 16384
TOTAL_PLUGINS = 32
N_MP = 8
DEVICES = 32


def shared_table(key):
    return jax.random.permutation(jax.random.fold_in(key, 11), TOTAL_PLUGINS).astype(jnp.int32)


def draw_slot_adapter_ids(key, part):
    return shared_table(key)


def draw_request_adapter(key, part):
    table = shared_table(key)
    device_count = REQUESTS // REQ_DEV
    scores = jax.random.randint(jax.random.fold_in(key, 12), (device_count, N_MP), 0, 1 << 20) * N_MP
    scores = scores + jnp.arange(N_MP, dtype=jnp.int32)[None, :]
    owners = jnp.argsort(scores, axis=1, stable=True)[:, :REQ_DEV].astype(jnp.int32)
    within = jax.random.randint(jax.random.fold_in(key, 13), (device_count, REQ_DEV), 0, APD)
    slot_ids = owners * APD + within
    return table[slot_ids].reshape(REQUESTS).astype(jnp.int32)


def draw_lengths(key, part):
    device_count = REQUESTS // REQ_DEV
    drawn = jax.random.randint(jax.random.fold_in(key, 21), (device_count, REQ_DEV), 1, SLOTR + 1)
    chosen = jax.random.randint(jax.random.fold_in(key, 22), (device_count, 1), 0, REQ_DEV)
    filled = jnp.where(jnp.arange(REQ_DEV)[None, :] == chosen, SLOTR, drawn)
    return filled.reshape(REQUESTS).astype(jnp.int32)


def draw_tokens(key, part):
    rest = jnp.clip(jax.random.normal(jax.random.fold_in(key, 31), (TOKENS, EMBED_SPAN), jnp.float32), -6.0, 6.0)
    return rest.astype(jnp.bfloat16)


def query_table(key):
    drawn = jax.random.normal(jax.random.fold_in(key, 41), (EMBED_SPAN, ATTN_CHANNELS), jnp.float32)
    return jnp.clip(drawn, -6.0, 6.0) * EMBED_SPAN ** (-0.5)


def draw_query_weight(key, part):
    return query_table(key).astype(jnp.bfloat16)


def draw_key_weight(key, part):
    drawn = jax.random.normal(jax.random.fold_in(key, 42), (EMBED_SPAN, ATTN_CHANNELS), jnp.float32)
    own = jnp.clip(drawn, -6.0, 6.0) * EMBED_SPAN ** (-0.5)
    return own.astype(jnp.bfloat16)


def steps_of(key, extent, shards, smallest, high):
    factor_of, own = 1.0, jax.random.fold_in(key, 6)
    for dim, blocks in shards:
        heights = jnp.exp(jax.random.uniform(jax.random.fold_in(own, dim), (blocks,), jnp.float32, smallest / len(shards), high / len(shards)))
        factor_of = factor_of * jnp.repeat(heights, extent[dim] // blocks).reshape([-1 if axis == dim else 1 for axis in range(len(extent))])
    return factor_of


def scatter_about(own_key, dims, scale, reach, split=(), kind=jnp.bfloat16):
    values = scale * jax.random.normal(own_key, dims, jnp.float32)
    if split:
        values = values * steps_of(own_key, dims, split, -0.22, 0.18)
    return jnp.clip(values, -reach, reach).astype(kind)


def setup_inputs(seed: int = 0) -> dict:
    keys = jax.random.split(jax.random.key(seed), 16)
    return {
        "tokens": draw_tokens(jax.random.fold_in(keys[15], 71), 0),
        "first_norm_gain": jnp.clip(1.0 + 0.15 * jax.random.normal(keys[1], (EMBED_SPAN,), jnp.float32), 0.25, 1.75),
        "query_weight": draw_query_weight(jax.random.fold_in(keys[15], 71), 0),
        "key_weight": draw_key_weight(jax.random.fold_in(keys[15], 71), 0),
        "value_weight": scatter_about(keys[4], (EMBED_SPAN, ATTN_CHANNELS), EMBED_SPAN ** -0.5, 0.125),
        "output_weight": scatter_about(keys[5], (ATTN_CHANNELS, EMBED_SPAN), ATTN_CHANNELS ** -0.5, 0.1875),
        "lengths": draw_lengths(jax.random.fold_in(keys[15], 71), 0),
        "request_adapter": draw_request_adapter(jax.random.fold_in(keys[15], 71), 0),
        "slot_adapter_ids": draw_slot_adapter_ids(jax.random.fold_in(keys[15], 71), 0),
        "plugin_shrink_maps": scatter_about(keys[9], (TOTAL_PLUGINS, EMBED_SPAN, 2 * LATENT_BREADTH), EMBED_SPAN ** -0.5, 0.125, ((0, 8),)),
        "plugin_grow_maps": scatter_about(keys[10], (TOTAL_PLUGINS, 2, LATENT_BREADTH, ATTN_CHANNELS), LATENT_BREADTH ** -0.5, 1.5, ((0, 8),)),
        "device_token_order": jax.vmap(lambda own: jax.random.permutation(own, TOK_DEV))(jax.random.split(keys[11], DEVICES)).reshape((DEVICES, TOK_DEV)).astype(jnp.int32),
        "second_norm_gain": jnp.clip(1.0 + 0.15 * jax.random.normal(keys[12], (EMBED_SPAN,), jnp.float32), 0.25, 1.75),
        "gate_weight": scatter_about(keys[13], (EMBED_SPAN, FF), EMBED_SPAN ** -0.5, 0.125, ((0, 32),)),
        "up_weight": scatter_about(keys[14], (EMBED_SPAN, FF), EMBED_SPAN ** -0.5, 0.125, ((0, 32),)),
    }


PLUGIN_STRENGTH = 2.0
EPSILON = 1e-05

def normalize(rows_in, gain_vec):
    floated = rows_in.astype(jnp.float32)
    scale = lax.rsqrt(lax.optimization_barrier(jnp.mean(floated * floated, axis=-1, keepdims=True)) + EPSILON)
    return (floated * scale * gain_vec.astype(jnp.float32)).astype(jnp.bfloat16)

def attend(query, key, value, request_len):
    queries = query.reshape(REQ_DEV, SLOTR, HEADS, HD).astype(jnp.float32)
    head_keys = key.reshape(REQ_DEV, SLOTR, HEADS, HD).astype(jnp.float32)
    head_values = value.reshape(REQ_DEV, SLOTR, HEADS, HD).astype(jnp.float32)
    scores = jnp.einsum('rqhd,rkhd->rhqk', queries, head_keys) * HD ** (-0.5)
    places = jnp.arange(SLOTR)
    query_place = places[:, None]
    key_place = places[None, :]
    allowed = (key_place <= query_place) & ((query_place - key_place < WINDOW) | (key_place < SINKS))
    key_live = places[None, :] < request_len[:, None]
    visible_lookup_flags = allowed[None, None, :, :] & key_live[:, None, None, :]
    scores = jnp.where(visible_lookup_flags, scores, -1e+30)
    row_max = lax.optimization_barrier(jnp.max(scores, axis=-1, keepdims=True))
    expo = jnp.where(visible_lookup_flags, jnp.exp(scores - row_max), 0.0)
    softmax_w = (expo / lax.optimization_barrier(jnp.sum(expo, axis=-1, keepdims=True))).astype(jnp.bfloat16)
    attended = jnp.einsum('rhqk,rkhd->rqhd', softmax_w.astype(jnp.float32), head_values).astype(jnp.bfloat16)
    query_live = (places[None, :] < request_len[:, None])[:, :, None, None]
    attended = jnp.where(query_live, attended, jnp.zeros_like(attended))
    return attended.reshape(REQ_DEV * SLOTR, HEADS * HD)

def reference(tokens, first_norm_gain, query_weight, key_weight, value_weight, output_weight, lengths, request_adapter, slot_adapter_ids, plugin_shrink_maps, plugin_grow_maps, device_token_order, second_norm_gain, gate_weight, up_weight):
    slot_of = jnp.zeros((TOTAL_PLUGINS,), jnp.int32).at[slot_adapter_ids].set(jnp.arange(TOTAL_PLUGINS, dtype=jnp.int32))
    slot_ids = slot_of[request_adapter].reshape(DEVICES, REQ_DEV)
    tok_dev = REQ_DEV * SLOTR
    hw_size = HEADS * HD

    def one_device(packed):
        rows_in, request_len, slots_per_device = packed
        normed = normalize(rows_in, first_norm_gain)
        down_matrices = plugin_shrink_maps[slots_per_device].astype(jnp.float32)
        growth_coefficients = plugin_grow_maps[slots_per_device].astype(jnp.float32)
        request_rows = normed.reshape(REQ_DEV, SLOTR, EMBED_SPAN).astype(jnp.float32)
        thin_latent_image = jnp.einsum('rsd,rdk->rsk', request_rows, down_matrices).astype(jnp.bfloat16).astype(jnp.float32)
        queries_lowrank_delta = (jnp.einsum('lce,lef->lcf', thin_latent_image[..., :LATENT_BREADTH], growth_coefficients[:, 0]) * PLUGIN_STRENGTH).astype(jnp.bfloat16)
        values_lowrank_delta = (jnp.einsum('lce,lef->lcf', thin_latent_image[..., LATENT_BREADTH:], growth_coefficients[:, 1]) * PLUGIN_STRENGTH).astype(jnp.bfloat16)
        query = (jnp.dot(normed, query_weight, preferred_element_type=jnp.float32) + queries_lowrank_delta.reshape(tok_dev, hw_size).astype(jnp.float32)).astype(jnp.bfloat16)
        key = jnp.dot(normed, key_weight, preferred_element_type=jnp.float32).astype(jnp.bfloat16)
        value = (jnp.dot(normed, value_weight, preferred_element_type=jnp.float32) + values_lowrank_delta.reshape(tok_dev, hw_size).astype(jnp.float32)).astype(jnp.bfloat16)
        attended = attend(query, key, value, request_len)
        mixed = rows_in.astype(jnp.float32) + jnp.dot(attended, output_weight, preferred_element_type=jnp.float32)
        return mixed.astype(jnp.bfloat16)
    residual = lax.map(one_device, (tokens.reshape(DEVICES, tok_dev, EMBED_SPAN), lengths.reshape(DEVICES, REQ_DEV), slot_ids))
    shuffled = jnp.take_along_axis(residual, device_token_order[:, :, None], axis=1)
    block_rows = tok_dev // DEVICES
    regrouped = shuffled.reshape(DEVICES, DEVICES, block_rows, EMBED_SPAN).transpose(1, 0, 2, 3)
    regrouped = regrouped.reshape(DEVICES, tok_dev, EMBED_SPAN)

    def gated(rows_in):
        mlp_input = normalize(rows_in, second_norm_gain)
        gate = jnp.dot(mlp_input, gate_weight, preferred_element_type=jnp.float32)
        upper = jnp.dot(mlp_input, up_weight, preferred_element_type=jnp.float32)
        return (jax.nn.silu(gate) * upper).astype(jnp.bfloat16)
    hidden = lax.map(gated, regrouped)
    return (residual.reshape(DEVICES * tok_dev, EMBED_SPAN), hidden.reshape(DEVICES * tok_dev, FF))
```

```python
import functools

import jax
import jax.numpy as jnp
from jax import lax
from jax.experimental import pallas as pl
from jax.experimental.pallas import tpu as pltpu
from jax.sharding import PartitionSpec as P

EMBED_SPAN = 1792
HEADS = 8
HD = 112
LATENT_BREADTH = 16
REQ_DEV = 8
TOK_DEV = 512
SLOTR = 64
WINDOW = 32
SINKS = 4


PLUGIN_STRENGTH = 2.0
EPSILON = 1e-05


def normalize(rows_in, gain_vec):
    floated = rows_in.astype(jnp.float32)
    scale = lax.rsqrt(jnp.mean(floated * floated, axis=-1, keepdims=True) + EPSILON)
    return (floated * scale * gain_vec).astype(jnp.bfloat16)


def attend(query, key, value, request_len):
    queries = query.reshape(REQ_DEV, SLOTR, HEADS, HD)
    head_keys = key.reshape(REQ_DEV, SLOTR, HEADS, HD)
    head_values = value.reshape(REQ_DEV, SLOTR, HEADS, HD)
    scores = jnp.einsum(
        "rqhd,rkhd->rhqk", queries, head_keys, preferred_element_type=jnp.float32
    ) * HD ** (-0.5)
    places = jnp.arange(SLOTR)
    query_place = places[:, None]
    key_place = places[None, :]
    allowed = (key_place <= query_place) & (
        (query_place - key_place < WINDOW) | (key_place < SINKS)
    )
    key_live = places[None, :] < request_len[:, None]
    visible_lookup_flags = allowed[None, None, :, :] & key_live[:, None, None, :]
    scores = jnp.where(visible_lookup_flags, scores, -1e30)
    row_max = jnp.max(scores, axis=-1, keepdims=True)
    expo = jnp.where(visible_lookup_flags, jnp.exp(scores - row_max), 0.0)
    softmax_w = (expo / jnp.sum(expo, axis=-1, keepdims=True)).astype(jnp.bfloat16)
    attended = jnp.einsum(
        "rhqk,rkhd->rqhd", softmax_w, head_values, preferred_element_type=jnp.float32
    ).astype(jnp.bfloat16)
    query_live = (places[None, :] < request_len[:, None])[:, :, None, None]
    attended = jnp.where(query_live, attended, jnp.zeros_like(attended))
    return attended.reshape(REQ_DEV * SLOTR, HEADS * HD)


CORES = 2


def gate_kernel(rows_ref, gain_ref, w_ref, act_ref, o_ref):
    @pl.when(pl.program_id(0) == 0)
    def _():
        @pl.loop(0, rows_ref.shape[0], step=64)
        def _(r):
            part = pl.ds(pl.multiple_of(r, 64), 64)
            wide = rows_ref[part, :].astype(jnp.float32)
            scale = lax.rsqrt(jnp.mean(wide * wide, axis=-1, keepdims=True) + EPSILON)
            act_ref[part, :] = (wide * scale * gain_ref[...]).astype(jnp.bfloat16)

    gate = jnp.dot(act_ref[...], w_ref[...], preferred_element_type=jnp.float32)
    o_ref[...] = gate * jax.nn.sigmoid(gate)


def gate_units(regrouped, gain, weight):
    rows, depth = regrouped.shape
    width = weight.shape[1]
    tile = 512
    whole = lambda i: (0, 0)
    strip = lambda i: (0, i)
    return pl.pallas_call(
        gate_kernel,
        out_shape=(
            jax.ShapeDtypeStruct((rows, depth), jnp.bfloat16),
            jax.ShapeDtypeStruct((rows, width), jnp.float32),
        ),
        grid=(width // tile,),
        in_specs=[
            pl.BlockSpec((rows, depth), whole),
            pl.BlockSpec((1, depth), whole),
            pl.BlockSpec((depth, tile), strip),
        ],
        out_specs=(pl.BlockSpec((rows, depth), whole), pl.BlockSpec((rows, tile), strip)),
        compiler_params=pltpu.CompilerParams(vmem_limit_bytes=32 << 20),
        name="gate_units",
    )(regrouped, gain[None, :], weight)


def up_kernel(act_ref, silu_ref, w_ref, o_ref):
    up = jnp.dot(act_ref[...], w_ref[...], preferred_element_type=jnp.float32)
    o_ref[...] = (silu_ref[...] * up).astype(o_ref.dtype)


def up_units(act, silu, weight):
    rows, depth = act.shape
    width = weight.shape[1]
    tile = 512
    strip = lambda i: (0, i)
    return pl.pallas_call(
        up_kernel,
        out_shape=jax.ShapeDtypeStruct((rows, width), jnp.bfloat16),
        grid=(width // tile,),
        in_specs=[
            pl.BlockSpec((rows, depth), lambda i: (0, 0)),
            pl.BlockSpec((rows, tile), strip),
            pl.BlockSpec((depth, tile), strip),
        ],
        out_specs=pl.BlockSpec((rows, tile), strip),
        compiler_params=pltpu.CompilerParams(vmem_limit_bytes=48 << 20),
        name="up_units",
    )(act, silu, weight)


def local_plain(
    tokens,
    first_norm_gain,
    query_weight,
    key_weight,
    value_weight,
    output_weight,
    lengths,
    request_adapter,
    slot_adapter_ids,
    plugin_shrink_maps,
    plugin_grow_maps,
    device_token_order,
    second_norm_gain,
    gate_weight,
    up_weight,
):
    owner_count = lax.axis_size("mp")
    resident_slots = plugin_shrink_maps.shape[0]
    tok_dev = tokens.shape[0]
    hw_size = query_weight.shape[1]
    every = ("x", "core", "mp")

    gate_full = lax.all_gather(gate_weight, every, axis=0, tiled=True)
    up_full = lax.all_gather(up_weight, every, axis=0, tiled=True)

    matches = (slot_adapter_ids[None, :] == request_adapter[:, None]).astype(jnp.int32)
    slot_ids = jnp.sum(
        matches * jnp.arange(slot_adapter_ids.shape[0], dtype=jnp.int32)[None, :], axis=1
    )
    owner_index = slot_ids // resident_slots
    within = slot_ids % resident_slots
    routing = (jnp.arange(owner_count)[:, None] == owner_index[None, :]).astype(jnp.bfloat16)
    slot_pick = (jnp.arange(resident_slots)[None, :] == within[:, None]).astype(jnp.bfloat16)
    chosen = jnp.dot(routing, slot_pick, preferred_element_type=jnp.float32).astype(jnp.bfloat16)
    chosen_adapter = lax.all_to_all(chosen, "mp", split_axis=0, concat_axis=0, tiled=True)
    maps = jnp.concatenate(
        [
            plugin_shrink_maps.transpose(0, 2, 1),
            plugin_grow_maps.reshape(resident_slots, 2 * LATENT_BREADTH, hw_size),
        ],
        axis=-1,
    )
    outgoing = jnp.einsum(
        "ge,ezc->gzc", chosen_adapter, maps, preferred_element_type=jnp.float32
    ).astype(jnp.bfloat16)
    incoming = lax.all_to_all(outgoing, "mp", split_axis=0, concat_axis=0, tiled=True)
    own_maps = jnp.einsum(
        "or,ozc->rzc", routing, incoming, preferred_element_type=jnp.float32
    ).astype(jnp.bfloat16)

    normed = normalize(tokens, first_norm_gain)
    request_rows = normed.reshape(REQ_DEV, SLOTR, EMBED_SPAN)
    codes = jnp.einsum(
        "rsd,rkd->rsk",
        request_rows,
        own_maps[..., :EMBED_SPAN],
        preferred_element_type=jnp.float32,
    ).astype(jnp.bfloat16)
    delta_q = (
        jnp.einsum(
            "rsk,rkh->rsh",
            codes[..., :LATENT_BREADTH],
            own_maps[:, :LATENT_BREADTH, EMBED_SPAN:],
            preferred_element_type=jnp.float32,
        )
        * PLUGIN_STRENGTH
    ).astype(jnp.bfloat16)
    delta_v = (
        jnp.einsum(
            "rsk,rkh->rsh",
            codes[..., LATENT_BREADTH:],
            own_maps[:, LATENT_BREADTH:, EMBED_SPAN:],
            preferred_element_type=jnp.float32,
        )
        * PLUGIN_STRENGTH
    ).astype(jnp.bfloat16)
    query = (
        jnp.dot(normed, query_weight, preferred_element_type=jnp.float32)
        + delta_q.reshape(tok_dev, hw_size).astype(jnp.float32)
    ).astype(jnp.bfloat16)
    key = jnp.dot(normed, key_weight, preferred_element_type=jnp.float32).astype(jnp.bfloat16)
    value = (
        jnp.dot(normed, value_weight, preferred_element_type=jnp.float32)
        + delta_v.reshape(tok_dev, hw_size).astype(jnp.float32)
    ).astype(jnp.bfloat16)
    attended = attend(query, key, value, lengths)
    residual = (
        tokens.astype(jnp.float32)
        + jnp.dot(attended, output_weight, preferred_element_type=jnp.float32)
    ).astype(jnp.bfloat16)
    order = device_token_order.reshape(-1, 1) == jnp.arange(tok_dev)[None, :]
    shuffled = jnp.dot(
        order.astype(jnp.bfloat16), residual, preferred_element_type=jnp.float32
    ).astype(jnp.bfloat16)
    regrouped = lax.all_to_all(shuffled, every, split_axis=0, concat_axis=0, tiled=True)
    act, silu = gate_units(regrouped, second_norm_gain, gate_full)
    hidden = up_units(act, silu, up_full)
    return (residual, hidden)


MESH = pl.DeviceIdType.MESH
STRIP = 256


def exchange_kernel(
    shape, spans, shuf, gate, up, out, stage, wide, rows, held,
    swap_send, swap_recv, swap_own, w_send, w_recv, r_send, r_recv, f_send, f_recv, o_own, o_send, o_recv,
):
    X, A, B = shape
    x, c, a, b = (lax.axis_index(n) for n in ("x", "core", "a", "b"))
    sib = {"core": 1 - c}
    sizes = {"x": X, "a": A, "b": B}
    mine = {"x": x, "a": a, "b": b}
    depth = gate.shape[0]
    half = wide.shape[2]
    chips = X * A * B

    def chip_of(at):
        return (at["x"] * A + at["a"]) * B + at["b"]

    def moved(at, axis, k):
        return {**at, axis: lax.rem(at[axis] + k, sizes[axis])}

    barrier = pltpu.get_barrier_semaphore()
    peers = []
    for i in range(X):
        for j in range(A):
            for k in range(B):
                if i or j or k:
                    peers.append(moved(moved(moved(mine, "x", i), "a", j), "b", k))
    pl.semaphore_signal(barrier, inc=1, device_id=sib, device_id_type=MESH)
    for p in peers:
        pl.semaphore_signal(barrier, inc=1, device_id=p, device_id_type=MESH)
    pl.semaphore_wait(barrier, chips)

    me = chip_of(mine)
    sends = []
    swaps = []
    for mat, w in enumerate((gate, up)):
        theirs = pl.ds(pl.multiple_of((1 - c) * half, half), half)
        ours = pl.ds(pl.multiple_of(c * half, half), half)
        s = pltpu.make_async_remote_copy(
            w.at[:, theirs], stage.at[mat, c], swap_send.at[mat], swap_recv.at[mat],
            device_id=sib, device_id_type=MESH,
        )
        s.start()
        l = pltpu.make_async_copy(w.at[:, ours], stage.at[mat, c], swap_own.at[mat])
        l.start()
        swaps.append((s, l))

    def row_copy(p, k):
        return pltpu.make_async_remote_copy(
            shuf.at[chip_of(p)], rows.at[:, x, c, a, b], r_send.at[k], r_recv.at[me],
            device_id=p, device_id_type=MESH,
        )

    for k, p in enumerate(peers):
        d = row_copy(p, k)
        d.start()
        sends.append(d)
    own_rows = pltpu.make_async_copy(shuf.at[me], rows.at[:, x, c, a, b], r_recv.at[me])
    own_rows.start()

    def forward_rows(p, k):
        here = rows.at[:, p["x"], c, p["a"], p["b"]]
        d = pltpu.make_async_remote_copy(
            here, here, f_send.at[k], f_recv.at[k], device_id=sib, device_id_type=MESH
        )
        d.start()
        sends.append(d)

    def slot(mat, span, chip):
        start, width = spans[span]
        return wide.at[
            mat, pl.ds(pl.multiple_of(chip * 2 * depth, 16), 2 * depth), pl.ds(start, width)
        ]

    count = [0]

    def send(mat, span, at, axis):
        ref = slot(mat, span, chip_of(at))
        for k in range(1, sizes[axis]):
            to = {axis: lax.rem(mine[axis] + k, sizes[axis])}
            d = pltpu.make_async_remote_copy(
                ref, ref, w_send.at[count[0]], w_recv.at[mat, span, chip_of(at)],
                device_id=to, device_id_type=MESH,
            )
            count[0] += 1
            d.start()
            sends.append(d)

    def arrived(mat, span, at):
        ref = slot(mat, span, chip_of(at))
        pltpu.make_async_remote_copy(
            ref, ref, w_send.at[0], w_recv.at[mat, span, chip_of(at)],
            device_id=sib, device_id_type=MESH,
        ).wait_recv()

    orders = (("x", "b"), ("b", "x"))
    for mat in range(2):
        s, l = swaps[mat]
        l.wait()
        s.wait()
        joined = jnp.concatenate(
            [stage[mat, 0].astype(jnp.float32), stage[mat, 1].astype(jnp.float32)], axis=0
        ).astype(jnp.bfloat16)
        wide[mat, pl.ds(pl.multiple_of(me * 2 * depth, 16), 2 * depth), :] = joined
    for span in range(len(spans)):
        for mat in range(2):
            second, third = orders[mat]
            send(mat, span, mine, "a")
            send(mat, span, mine, second)
            send(mat, span, mine, third)

    def near(span, j):
        at = moved(mine, "a", j)
        for mat in range(2):
            second, third = orders[mat]
            if j:
                arrived(mat, span, at)
                send(mat, span, at, second)
                send(mat, span, at, third)

    def middle(span, j):
        for mat in range(2):
            second, third = orders[mat]
            for k in range(1, sizes[second]):
                at = moved(moved(mine, "a", j), second, k)
                arrived(mat, span, at)
                send(mat, span, at, third)

    def far(span):
        for mat in range(2):
            second, third = orders[mat]
            for j in range(A):
                for i in range(sizes[second]):
                    for k in range(1, sizes[third]):
                        arrived(mat, span, moved(moved(moved(mine, "a", j), second, i), third, k))

    own_rows.wait()
    forward_rows(mine, chips - 1)
    line = [0] + [k for k in range(1, A)]
    for span in range(len(spans)):
        near(span, line[0])
        for i in range(1, A):
            near(span, line[i])
            middle(span, line[i - 1])
        middle(span, line[A - 1])
        if span == 0:
            for k, p in enumerate(peers):
                here = rows.at[:, p["x"], c, p["a"], p["b"]]
                pltpu.make_async_remote_copy(
                    here, here, r_send.at[k], r_recv.at[chip_of(p)],
                    device_id=sib, device_id_type=MESH,
                ).wait_recv()
                forward_rows(p, k)
    for k, p in enumerate(peers + [mine]):
        here = rows.at[:, p["x"], 1 - c, p["a"], p["b"]]
        pltpu.make_async_remote_copy(
            here, here, f_send.at[k], f_recv.at[k], device_id=sib, device_id_type=MESH
        ).wait_recv()

    def result(strip, part):
        cols = pl.ds(pl.multiple_of(c * half + strip * STRIP, STRIP), STRIP)
        at = lax.rem(strip, 2)
        if part == 0:
            return pltpu.make_async_remote_copy(
                held.at[at, 0], out.at[:, cols], o_send.at[at], o_recv.at[strip],
                device_id=sib, device_id_type=MESH,
            )
        return pltpu.make_async_copy(held.at[at, 1], out.at[:, cols], o_own.at[at])

    total = rows.shape[1] * 2 * A * B * rows.shape[5]

    def strip_step(strip, carry):
        @pl.when(strip >= 2)
        def _():
            result(strip - 2, 0).wait_send()
            result(strip - 2, 1).wait()

        cols = pl.ds(pl.multiple_of(strip * STRIP, STRIP), STRIP)
        for part in range(2):
            who = 1 - c if part == 0 else c
            act = rows[who].reshape(total, rows.shape[6])
            g = jnp.dot(act, wide[0, :, cols], preferred_element_type=jnp.float32)
            u = jnp.dot(act, wide[1, :, cols], preferred_element_type=jnp.float32)
            held[lax.rem(strip, 2), part] = (g * jax.nn.sigmoid(g) * u).astype(jnp.bfloat16)
            result(strip, part).start()
        return carry

    for span, (start, width) in enumerate(spans):
        far(span)
        lax.fori_loop(start // STRIP, (start + width) // STRIP, strip_step, 0)
    strips = half // STRIP
    for s in (strips - 2, strips - 1):
        result(jnp.int32(s), 0).wait_send()
        result(jnp.int32(s), 1).wait()
    for s in range(strips):
        result(jnp.int32(s), 0).wait_recv()
    for d in sends:
        d.wait_send()


def exchange(shape, shuf, gate_weight, up_weight):
    X, A, B = shape
    chips = X * A * B
    block, depth = shuf.shape[2:]
    shard, width = gate_weight.shape
    half = width // CORES
    spans = ((0, 768), (768, half - 768))
    DMA = pltpu.SemaphoreType.DMA
    return pl.pallas_call(
        functools.partial(exchange_kernel, shape, spans),
        out_shape=jax.ShapeDtypeStruct((chips * CORES * block, width), jnp.bfloat16),
        in_specs=[pl.BlockSpec(memory_space=pltpu.VMEM)] + [pl.BlockSpec(memory_space=pl.ANY)] * 2,
        out_specs=pl.BlockSpec(memory_space=pl.ANY),
        scratch_shapes=[
            pltpu.VMEM((2, CORES, shard, half), jnp.bfloat16),
            pltpu.VMEM((2, depth, half), jnp.bfloat16),
            pltpu.VMEM((CORES, X, CORES, A, B, block, depth), jnp.bfloat16),
            pltpu.VMEM((2, 2, chips * CORES * block, STRIP), jnp.bfloat16),
            DMA((2,)), DMA((2,)), DMA((2,)),
            DMA((2 * len(spans) * (chips - 1),)), DMA((2, len(spans), chips)),
            DMA((chips,)), DMA((chips,)), DMA((chips,)), DMA((chips,)),
            DMA((2,)), DMA((2,)), DMA((half // STRIP,)),
        ],
        compiler_params=pltpu.CompilerParams(
            collective_id=0, has_side_effects=True, vmem_limit_bytes=48 << 20
        ),
        name="exchange",
    )(shuf, gate_weight, up_weight)


def local_fused(
    tokens,
    first_norm_gain,
    query_weight,
    key_weight,
    value_weight,
    output_weight,
    lengths,
    request_adapter,
    slot_adapter_ids,
    plugin_shrink_maps,
    plugin_grow_maps,
    device_token_order,
    second_norm_gain,
    gate_weight,
    up_weight,
):
    owner_count = lax.axis_size(("a", "b"))
    resident_slots = plugin_shrink_maps.shape[0]
    tok_dev = tokens.shape[0]
    hw_size = query_weight.shape[1]
    every = ("x", "core", "a", "b")

    matches = (slot_adapter_ids[None, :] == request_adapter[:, None]).astype(jnp.int32)
    slot_ids = jnp.sum(
        matches * jnp.arange(slot_adapter_ids.shape[0], dtype=jnp.int32)[None, :], axis=1
    )
    owner_index = slot_ids // resident_slots
    within = slot_ids % resident_slots
    routing = (jnp.arange(owner_count)[:, None] == owner_index[None, :]).astype(jnp.bfloat16)
    slot_pick = (jnp.arange(resident_slots)[None, :] == within[:, None]).astype(jnp.bfloat16)
    chosen = jnp.dot(routing, slot_pick, preferred_element_type=jnp.float32).astype(jnp.bfloat16)
    chosen_adapter = lax.all_to_all(chosen, ("a", "b"), split_axis=0, concat_axis=0, tiled=True)
    maps = jnp.concatenate(
        [
            plugin_shrink_maps.transpose(0, 2, 1),
            plugin_grow_maps.reshape(resident_slots, 2 * LATENT_BREADTH, hw_size),
        ],
        axis=-1,
    )
    outgoing = jnp.einsum(
        "ge,ezc->gzc", chosen_adapter, maps, preferred_element_type=jnp.float32
    ).astype(jnp.bfloat16)
    incoming = lax.all_to_all(outgoing, ("a", "b"), split_axis=0, concat_axis=0, tiled=True)
    own_maps = jnp.einsum(
        "or,ozc->rzc", routing, incoming, preferred_element_type=jnp.float32
    ).astype(jnp.bfloat16)

    normed = normalize(tokens, first_norm_gain)
    request_rows = normed.reshape(REQ_DEV, SLOTR, EMBED_SPAN)
    codes = jnp.einsum(
        "rsd,rkd->rsk",
        request_rows,
        own_maps[..., :EMBED_SPAN],
        preferred_element_type=jnp.float32,
    ).astype(jnp.bfloat16)
    delta_q = (
        jnp.einsum(
            "rsk,rkh->rsh",
            codes[..., :LATENT_BREADTH],
            own_maps[:, :LATENT_BREADTH, EMBED_SPAN:],
            preferred_element_type=jnp.float32,
        )
        * PLUGIN_STRENGTH
    ).astype(jnp.bfloat16)
    delta_v = (
        jnp.einsum(
            "rsk,rkh->rsh",
            codes[..., LATENT_BREADTH:],
            own_maps[:, LATENT_BREADTH:, EMBED_SPAN:],
            preferred_element_type=jnp.float32,
        )
        * PLUGIN_STRENGTH
    ).astype(jnp.bfloat16)
    query = (
        jnp.dot(normed, query_weight, preferred_element_type=jnp.float32)
        + delta_q.reshape(tok_dev, hw_size).astype(jnp.float32)
    ).astype(jnp.bfloat16)
    key = jnp.dot(normed, key_weight, preferred_element_type=jnp.float32).astype(jnp.bfloat16)
    value = (
        jnp.dot(normed, value_weight, preferred_element_type=jnp.float32)
        + delta_v.reshape(tok_dev, hw_size).astype(jnp.float32)
    ).astype(jnp.bfloat16)
    attended = attend(query, key, value, lengths)
    residual = (
        tokens.astype(jnp.float32)
        + jnp.dot(attended, output_weight, preferred_element_type=jnp.float32)
    ).astype(jnp.bfloat16)
    shape = tuple(lax.axis_size(n) for n in ("x", "a", "b"))
    chips = shape[0] * shape[1] * shape[2]
    block = tok_dev // (chips * CORES)
    want = device_token_order.reshape(shape[0], CORES, -1, block).transpose(0, 2, 1, 3).reshape(-1, 1)
    order = want == jnp.arange(tok_dev)[None, :]
    act = normalize(residual, second_norm_gain)
    act = act.reshape(tok_dev, shape[0], CORES, shape[1] * shape[2], -1).transpose(0, 1, 3, 2, 4)
    shuffled = jnp.dot(
        order.astype(jnp.bfloat16), act.reshape(tok_dev, -1), preferred_element_type=jnp.float32
    ).astype(jnp.bfloat16)
    hidden = exchange(shape, shuffled.reshape(chips, CORES, block, -1), gate_weight, up_weight)
    return (residual, hidden)


def solution(mesh):
    dp, mp = mesh.devices.shape
    fast = 1
    while fast * fast * 4 <= mp:
        fast *= 2
    devices = dp * mp
    fits = EMBED_SPAN // devices * CORES % 16 == 0 and TOK_DEV // devices % 16 == 0
    if fits:
        names = ("a", "b")
        fine = jax.sharding.Mesh(
            mesh.devices.reshape(dp // CORES, CORES, mp // fast, fast), ("x", "core", "a", "b")
        )
    else:
        names = ("mp",)
        fine = jax.sharding.Mesh(
            mesh.devices.reshape(dp // CORES, CORES, mp), ("x", "core", "mp")
        )
    rows = ("x", "core") + names
    return jax.shard_map(
        local_fused if fits else local_plain,
        mesh=fine,
        in_specs=(
            P(rows, None),
            P(),
            P(),
            P(),
            P(),
            P(),
            P(rows),
            P(rows),
            P(),
            P(names, None, None),
            P(names, None, None, None),
            P(rows, None),
            P(),
            P(rows, None),
            P(rows, None),
        ),
        out_specs=(P(rows, None), P(rows, None)),
        check_vma=False,
    )
```

```python
import functools

import jax
import jax.numpy as jnp
import numpy as np
from jax import lax
from jax.experimental import pallas as pl
from jax.experimental.pallas import tpu as pltpu
from jax.sharding import PartitionSpec as P

EMBED_SPAN = 1792
HEADS = 8
HD = 112
LATENT_BREADTH = 16
REQ_DEV = 8
TOK_DEV = 512
APD = 4
SLOTR = 64
WINDOW = 32
SINKS = 4


PLUGIN_STRENGTH = 2.0
EPSILON = 1e-05


def normalize(rows_in, gain_vec):
    floated = rows_in.astype(jnp.float32)
    scale = lax.rsqrt(jnp.mean(floated * floated, axis=-1, keepdims=True) + EPSILON)
    return (floated * scale * gain_vec).astype(jnp.bfloat16)


def attend(query, key, value, request_len):
    queries = query.reshape(REQ_DEV, SLOTR, HEADS, HD)
    head_keys = key.reshape(REQ_DEV, SLOTR, HEADS, HD)
    head_values = value.reshape(REQ_DEV, SLOTR, HEADS, HD)
    scores = jnp.einsum(
        "rqhd,rkhd->rhqk", queries, head_keys, preferred_element_type=jnp.float32
    ) * HD ** (-0.5)
    places = jnp.arange(SLOTR)
    query_place = places[:, None]
    key_place = places[None, :]
    allowed = (key_place <= query_place) & (
        (query_place - key_place < WINDOW) | (key_place < SINKS)
    )
    key_live = places[None, :] < request_len[:, None]
    visible_lookup_flags = allowed[None, None, :, :] & key_live[:, None, None, :]
    scores = jnp.where(visible_lookup_flags, scores, -1e30)
    row_max = jnp.max(scores, axis=-1, keepdims=True)
    expo = jnp.where(visible_lookup_flags, jnp.exp(scores - row_max), 0.0)
    softmax_w = (expo / jnp.sum(expo, axis=-1, keepdims=True)).astype(jnp.bfloat16)
    attended = jnp.einsum(
        "rhqk,rkhd->rqhd", softmax_w, head_values, preferred_element_type=jnp.float32
    ).astype(jnp.bfloat16)
    query_live = (places[None, :] < request_len[:, None])[:, :, None, None]
    attended = jnp.where(query_live, attended, jnp.zeros_like(attended))
    return attended.reshape(REQ_DEV * SLOTR, HEADS * HD)


CORES = 2


def gate_kernel(rows_ref, gain_ref, w_ref, act_ref, o_ref):
    @pl.when(pl.program_id(0) == 0)
    def _():
        @pl.loop(0, rows_ref.shape[0], step=64)
        def _(r):
            part = pl.ds(pl.multiple_of(r, 64), 64)
            wide = rows_ref[part, :].astype(jnp.float32)
            scale = lax.rsqrt(jnp.mean(wide * wide, axis=-1, keepdims=True) + EPSILON)
            act_ref[part, :] = (wide * scale * gain_ref[...]).astype(jnp.bfloat16)

    gate = jnp.dot(act_ref[...], w_ref[...], preferred_element_type=jnp.float32)
    o_ref[...] = gate * jax.nn.sigmoid(gate)


def gate_units(regrouped, gain, weight):
    rows, depth = regrouped.shape
    width = weight.shape[1]
    tile = 512
    whole = lambda i: (0, 0)
    strip = lambda i: (0, i)
    return pl.pallas_call(
        gate_kernel,
        out_shape=(
            jax.ShapeDtypeStruct((rows, depth), jnp.bfloat16),
            jax.ShapeDtypeStruct((rows, width), jnp.float32),
        ),
        grid=(width // tile,),
        in_specs=[
            pl.BlockSpec((rows, depth), whole),
            pl.BlockSpec((1, depth), whole),
            pl.BlockSpec((depth, tile), strip),
        ],
        out_specs=(pl.BlockSpec((rows, depth), whole), pl.BlockSpec((rows, tile), strip)),
        compiler_params=pltpu.CompilerParams(vmem_limit_bytes=32 << 20),
        name="gate_units",
    )(regrouped, gain[None, :], weight)


def up_kernel(act_ref, silu_ref, w_ref, o_ref):
    up = jnp.dot(act_ref[...], w_ref[...], preferred_element_type=jnp.float32)
    o_ref[...] = (silu_ref[...] * up).astype(o_ref.dtype)


def up_units(act, silu, weight):
    rows, depth = act.shape
    width = weight.shape[1]
    tile = 512
    strip = lambda i: (0, i)
    return pl.pallas_call(
        up_kernel,
        out_shape=jax.ShapeDtypeStruct((rows, width), jnp.bfloat16),
        grid=(width // tile,),
        in_specs=[
            pl.BlockSpec((rows, depth), lambda i: (0, 0)),
            pl.BlockSpec((rows, tile), strip),
            pl.BlockSpec((depth, tile), strip),
        ],
        out_specs=pl.BlockSpec((rows, tile), strip),
        compiler_params=pltpu.CompilerParams(vmem_limit_bytes=48 << 20),
        name="up_units",
    )(act, silu, weight)


def local_plain(
    tokens,
    first_norm_gain,
    query_weight,
    key_weight,
    value_weight,
    output_weight,
    lengths,
    request_adapter,
    slot_adapter_ids,
    plugin_shrink_maps,
    plugin_grow_maps,
    device_token_order,
    second_norm_gain,
    gate_weight,
    up_weight,
):
    owner_count = lax.axis_size("mp")
    resident_slots = plugin_shrink_maps.shape[0]
    tok_dev = tokens.shape[0]
    hw_size = query_weight.shape[1]
    every = ("x", "core", "mp")

    gate_full = lax.all_gather(gate_weight, every, axis=0, tiled=True)
    up_full = lax.all_gather(up_weight, every, axis=0, tiled=True)

    matches = (slot_adapter_ids[None, :] == request_adapter[:, None]).astype(jnp.int32)
    slot_ids = jnp.sum(
        matches * jnp.arange(slot_adapter_ids.shape[0], dtype=jnp.int32)[None, :], axis=1
    )
    owner_index = slot_ids // resident_slots
    within = slot_ids % resident_slots
    routing = (jnp.arange(owner_count)[:, None] == owner_index[None, :]).astype(jnp.bfloat16)
    slot_pick = (jnp.arange(resident_slots)[None, :] == within[:, None]).astype(jnp.bfloat16)
    chosen = jnp.dot(routing, slot_pick, preferred_element_type=jnp.float32).astype(jnp.bfloat16)
    chosen_adapter = lax.all_to_all(chosen, "mp", split_axis=0, concat_axis=0, tiled=True)
    maps = jnp.concatenate(
        [
            plugin_shrink_maps.transpose(0, 2, 1),
            plugin_grow_maps.reshape(resident_slots, 2 * LATENT_BREADTH, hw_size),
        ],
        axis=-1,
    )
    outgoing = jnp.einsum(
        "ge,ezc->gzc", chosen_adapter, maps, preferred_element_type=jnp.float32
    ).astype(jnp.bfloat16)
    incoming = lax.all_to_all(outgoing, "mp", split_axis=0, concat_axis=0, tiled=True)
    own_maps = jnp.einsum(
        "or,ozc->rzc", routing, incoming, preferred_element_type=jnp.float32
    ).astype(jnp.bfloat16)

    normed = normalize(tokens, first_norm_gain)
    request_rows = normed.reshape(REQ_DEV, SLOTR, EMBED_SPAN)
    codes = jnp.einsum(
        "rsd,rkd->rsk",
        request_rows,
        own_maps[..., :EMBED_SPAN],
        preferred_element_type=jnp.float32,
    ).astype(jnp.bfloat16)
    delta_q = (
        jnp.einsum(
            "rsk,rkh->rsh",
            codes[..., :LATENT_BREADTH],
            own_maps[:, :LATENT_BREADTH, EMBED_SPAN:],
            preferred_element_type=jnp.float32,
        )
        * PLUGIN_STRENGTH
    ).astype(jnp.bfloat16)
    delta_v = (
        jnp.einsum(
            "rsk,rkh->rsh",
            codes[..., LATENT_BREADTH:],
            own_maps[:, LATENT_BREADTH:, EMBED_SPAN:],
            preferred_element_type=jnp.float32,
        )
        * PLUGIN_STRENGTH
    ).astype(jnp.bfloat16)
    query = (
        jnp.dot(normed, query_weight, preferred_element_type=jnp.float32)
        + delta_q.reshape(tok_dev, hw_size).astype(jnp.float32)
    ).astype(jnp.bfloat16)
    key = jnp.dot(normed, key_weight, preferred_element_type=jnp.float32).astype(jnp.bfloat16)
    value = (
        jnp.dot(normed, value_weight, preferred_element_type=jnp.float32)
        + delta_v.reshape(tok_dev, hw_size).astype(jnp.float32)
    ).astype(jnp.bfloat16)
    attended = attend(query, key, value, lengths)
    residual = (
        tokens.astype(jnp.float32)
        + jnp.dot(attended, output_weight, preferred_element_type=jnp.float32)
    ).astype(jnp.bfloat16)
    order = device_token_order.reshape(-1, 1) == jnp.arange(tok_dev)[None, :]
    shuffled = jnp.dot(
        order.astype(jnp.bfloat16), residual, preferred_element_type=jnp.float32
    ).astype(jnp.bfloat16)
    regrouped = lax.all_to_all(shuffled, every, split_axis=0, concat_axis=0, tiled=True)
    act, silu = gate_units(regrouped, second_norm_gain, gate_full)
    hidden = up_units(act, silu, up_full)
    return (residual, hidden)


MESH = pl.DeviceIdType.MESH
STRIP = 256
PAIR = 2 * SLOTR
LANES = 128
NEVER = -1e30


def layer_kernel(
    shape, spans,
    slots, lens, tokens, wq, wk, wv, wo, shrink, grow, gate, up, gain1, gain2, want, source,
    res_out, hid_out,
    tok, wqkv, wout, normed, qf, vf, kb, qb, vb, att, act, shuf,
    ads, adg, stage, wide, rows, held,
    load_sem, ad_sem, swap_send, swap_recv, swap_own, i_send, i_recv, m_send, m_recv,
    r_send, r_recv, f_send, f_recv, o_own, o_send, o_recv, res_sem,
):
    X, A, B = shape
    x, c, a, b = (lax.axis_index(n) for n in ("x", "core", "a", "b"))
    sib = {"core": 1 - c}
    sizes = {"x": X, "a": A, "b": B}
    mine = {"x": x, "a": a, "b": b}
    depth = gate.shape[0]
    half = wide.shape[2]
    chips = X * A * B
    tok_dev = tok.shape[0]
    span_embed = tok.shape[1]
    heads_wide = kb.shape[1]
    f32 = jnp.float32
    bf16 = jnp.bfloat16

    def chip_of(at):
        return (at["x"] * A + at["a"]) * B + at["b"]

    def moved(at, axis, k):
        return {**at, axis: lax.rem(at[axis] + k, sizes[axis])}

    me = chip_of(mine)
    which = x * CORES + c
    loads = []
    own_ads = []
    for k, (frm, to) in enumerate(((shrink, ads), (grow, adg))):
        d = pltpu.make_async_copy(frm.at[which], to.at[c, me], ad_sem.at[k])
        d.start()
        own_ads.append(d)
    for k, (frm, to) in enumerate(
        ((tokens, tok), (wk, wqkv.at[1]), (wq, wqkv.at[0]), (wv, wqkv.at[2]), (wo, wout))
    ):
        d = pltpu.make_async_copy(frm, to, load_sem.at[k])
        d.start()
        loads.append(d)
    theirs = pl.ds(pl.multiple_of((1 - c) * half, half), half)
    ours = pl.ds(pl.multiple_of(c * half, half), half)
    own_halves = []
    for mat, w in enumerate((gate, up)):
        d = pltpu.make_async_copy(w.at[:, ours], stage.at[mat, c], swap_own.at[mat])
        d.start()
        own_halves.append(d)

    barrier = pltpu.get_barrier_semaphore()
    peers = []
    for i in range(X):
        for j in range(A):
            for k in range(B):
                if i or j or k:
                    peers.append(moved(moved(moved(mine, "x", i), "a", j), "b", k))
    pl.semaphore_signal(barrier, inc=1, device_id=sib, device_id_type=MESH)
    for p in peers:
        pl.semaphore_signal(barrier, inc=1, device_id=p, device_id_type=MESH)
    pl.semaphore_wait(barrier, chips)

    sends = []
    swaps = []
    for mat, w in enumerate((gate, up)):
        s = pltpu.make_async_remote_copy(
            w.at[:, theirs], stage.at[mat, c], swap_send.at[mat], swap_recv.at[mat],
            device_id=sib, device_id_type=MESH,
        )
        s.start()
        swaps.append(s)

    def weight_slot(mat, span):
        start, width = spans[span]

        def get(chip):
            at = pl.ds(pl.multiple_of(chip * 2 * depth, 16), 2 * depth)
            return wide.at[mat, at, pl.ds(start, width)]

        return get

    items = [
        (lambda chip: ads.at[c, chip], ("b", "x")),
        (lambda chip: adg.at[c, chip], ("x", "b")),
    ]
    ADAPT = (0, 1)
    weights = []
    for span in range(len(spans)):
        weights.append((len(items), len(items) + 1))
        items.append((weight_slot(0, span), ("x", "b")))
        items.append((weight_slot(1, span), ("b", "x")))
    count = [0]

    def send(n, at, axis):
        ref = items[n][0](chip_of(at))
        for k in range(1, sizes[axis]):
            d = pltpu.make_async_remote_copy(
                ref, ref, i_send.at[count[0]], i_recv.at[n, chip_of(at)],
                device_id={axis: lax.rem(mine[axis] + k, sizes[axis])}, device_id_type=MESH,
            )
            count[0] += 1
            d.start()
            sends.append(d)

    def arrived(n, at):
        ref = items[n][0](chip_of(at))
        pltpu.make_async_remote_copy(
            ref, ref, i_send.at[0], i_recv.at[n, chip_of(at)], device_id=sib, device_id_type=MESH
        ).wait_recv()

    def start_line(ns):
        for n in ns:
            send(n, mine, "a")

    def start_rest(ns):
        for n in ns:
            for axis in items[n][1]:
                send(n, mine, axis)

    def near(ns, j):
        for n in ns:
            at = moved(mine, "a", j)
            arrived(n, at)
            for axis in items[n][1]:
                send(n, at, axis)

    def middle(ns, j):
        for n in ns:
            second, third = items[n][1]
            for k in range(1, sizes[second]):
                at = moved(moved(mine, "a", j), second, k)
                arrived(n, at)
                send(n, at, third)

    def far(ns):
        for n in ns:
            second, third = items[n][1]
            for j in range(A):
                for i in range(sizes[second]):
                    for k in range(1, sizes[third]):
                        arrived(n, moved(moved(moved(mine, "a", j), second, i), third, k))

    for d in own_ads:
        d.wait()
    start_line(ADAPT)
    start_rest(ADAPT)
    for mat in range(2):
        own_halves[mat].wait()
        swaps[mat].wait()
        joined = jnp.concatenate(
            [stage[mat, 0].astype(f32), stage[mat, 1].astype(f32)], axis=0
        ).astype(bf16)
        wide[mat, pl.ds(pl.multiple_of(me * 2 * depth, 16), 2 * depth), :] = joined
    start_line(weights[0])

    loads[0].wait()

    @pl.loop(0, tok_dev, step=PAIR)
    def _(r):
        part = pl.ds(pl.multiple_of(r, PAIR), PAIR)
        wf = tok[part, :].astype(f32)
        scale = lax.rsqrt(jnp.mean(wf * wf, axis=-1, keepdims=True) + EPSILON)
        normed[part, :] = (wf * scale * gain1[...]).astype(bf16)

    def project(k, to):
        @pl.loop(0, tok_dev, step=256)
        def _(r):
            part = pl.ds(pl.multiple_of(r, 256), 256)
            to[part, :] = jnp.dot(
                normed[part, :], wqkv[k], preferred_element_type=f32
            ).astype(to.dtype)

    for j in range(1, A):
        near(ADAPT, j)
        if j == 1:
            start_rest(weights[0])
    loads[1].wait()
    project(1, kb)
    for j in range(A):
        middle(ADAPT, j)
    loads[2].wait()
    project(0, qf)
    for j in range(1, A):
        near(weights[0], j)
    loads[3].wait()
    project(2, vf)
    far(ADAPT)
    shares = []
    for k, ref in enumerate((ads, adg)):
        d = pltpu.make_async_remote_copy(
            ref.at[c], ref.at[c], m_send.at[k], m_recv.at[k], device_id=sib, device_id_type=MESH
        )
        d.start()
        shares.append(d)
    middle(weights[0], 0)
    for later in weights[1:]:
        start_line(later)
        start_rest(later)
    for j in range(1, A):
        middle(weights[0], j)
    for d in shares:
        d.wait()

    column = lax.broadcasted_iota(jnp.int32, (1, heads_wide), 1)

    def pair_step(pair, carry):
        for n in range(2):
            r = pair * 2 + n
            part = pl.ds(pl.multiple_of(r * SLOTR, SLOTR), SLOTR)
            slot = slots[r]
            codes = lax.dot_general(
                normed[part, :], ads[slot % CORES, slot // CORES],
                (((1,), (1,)), ((), ())), preferred_element_type=f32,
            ).astype(bf16)
            g = adg[slot % CORES, slot // CORES]
            lane = lax.broadcasted_iota(jnp.int32, codes.shape, 1)
            none = jnp.zeros_like(codes)
            for low, base, to in ((True, qf, qb), (False, vf, vb)):
                kept = jnp.where((lane < LATENT_BREADTH) == low, codes, none)
                delta = jnp.dot(kept, g, preferred_element_type=f32) * PLUGIN_STRENGTH
                to[part, :] = (base[part, :] + delta.astype(bf16).astype(f32)).astype(bf16)
        part = pl.ds(pl.multiple_of(pair * PAIR, PAIR), PAIR)
        i = lax.broadcasted_iota(jnp.int32, (PAIR, PAIR), 0)
        j = lax.broadcasted_iota(jnp.int32, (PAIR, PAIR), 1)
        len0, len1 = lens[pair * 2], lens[pair * 2 + 1]
        qi = jnp.where(i < SLOTR, i, i - SLOTR)
        kj = jnp.where(j < SLOTR, j, j - SLOTR)
        same = (i < SLOTR) == (j < SLOTR)
        live = kj < jnp.where(j < SLOTR, len0, len1)
        seen = same & live & (kj <= qi) & ((qi - kj < WINDOW) | (kj < SINKS))
        row = lax.broadcasted_iota(jnp.int32, (PAIR, 1), 0)
        alive = jnp.where(row < SLOTR, row, row - SLOTR) < jnp.where(row < SLOTR, len0, len1)
        before = None
        for h in range(HEADS):
            lo, hi = h * HD, (h + 1) * HD
            first, last = lo // LANES, (hi - 1) // LANES
            cols = slice(first * LANES, (last + 1) * LANES)
            q = qb[part, cols]
            pick = (column[:, cols] >= lo) & (column[:, cols] < hi)
            q = jnp.where(pick, q, jnp.zeros_like(q))
            s = lax.dot_general(
                q, kb[part, cols], (((1,), (1,)), ((), ())), preferred_element_type=f32
            ) * HD ** (-0.5)
            s = jnp.where(seen, s, NEVER)
            e = jnp.where(seen, jnp.exp(s - jnp.max(s, axis=-1, keepdims=True)), 0.0)
            p = (e / jnp.sum(e, axis=-1, keepdims=True)).astype(bf16)
            o = jnp.dot(p, vb[part, cols], preferred_element_type=f32)
            o = jnp.where(alive, o, 0.0).astype(bf16)
            if h > 0:
                w = h - 1
                at = column[:, w * LANES:(w + 1) * LANES]
                att[part, w * LANES:(w + 1) * LANES] = jnp.where(at < lo, before, o[:, :LANES])
            before = o[:, -LANES:]
        return carry

    quarter = tok_dev // PAIR // 4 or 1
    steps = tok_dev // PAIR
    for n in range(0, steps, quarter):
        lax.fori_loop(n, n + quarter, pair_step, 0)
        step = n // quarter
        for later in weights[1:]:
            if step + 1 < A:
                near(later, step + 1)
            if step < A:
                middle(later, step)
    loads[4].wait()

    group = source.shape[1]
    ahead = lax.broadcasted_iota(jnp.int32, (group, group), 0)
    turn = jnp.where(ahead == source[...], 1.0, 0.0).astype(bf16)

    @pl.loop(0, tok_dev, step=PAIR)
    def _(r):
        part = pl.ds(pl.multiple_of(r, PAIR), PAIR)
        mixed = tok[part, :].astype(f32) + jnp.dot(
            att[part, :], wout[...], preferred_element_type=f32
        )
        mixed = mixed.astype(bf16)
        tok[part, :] = mixed
        wf = mixed.astype(f32)
        scale = lax.rsqrt(jnp.mean(wf * wf, axis=-1, keepdims=True) + EPSILON)
        nb = (wf * scale * gain2[...]).astype(bf16)
        for g in range(span_embed // group):
            cols = slice(g * group, (g + 1) * group)
            act[part, cols] = jnp.dot(nb[:, cols], turn, preferred_element_type=f32).astype(bf16)

    res = pltpu.make_async_copy(tok, res_out, res_sem.at[0])
    res.start()
    block = rows.shape[5]
    per = 4
    lanes = lax.broadcasted_iota(jnp.int32, (per * CORES * block, tok_dev), 1)

    @pl.loop(0, chips // per)
    def _(n):
        size = per * CORES * block
        pick = want[pl.ds(pl.multiple_of(n * size, size), size), :]
        one = jnp.where(lanes == pick, 1.0, 0.0).astype(bf16)
        moved_rows = jnp.dot(one, act[...], preferred_element_type=f32).astype(bf16)
        shuf[pl.ds(n * per, per)] = moved_rows.reshape(per, CORES, block, span_embed)

    for k, p in enumerate(peers):
        d = pltpu.make_async_remote_copy(
            shuf.at[chip_of(p)], rows.at[:, x, c, a, b], r_send.at[k], r_recv.at[me],
            device_id=p, device_id_type=MESH,
        )
        d.start()
        sends.append(d)
    own_rows = pltpu.make_async_copy(shuf.at[me], rows.at[:, x, c, a, b], r_recv.at[me])
    own_rows.start()

    def forward_rows(p, k):
        here = rows.at[:, p["x"], c, p["a"], p["b"]]
        d = pltpu.make_async_remote_copy(
            here, here, f_send.at[k], f_recv.at[k], device_id=sib, device_id_type=MESH
        )
        d.start()
        sends.append(d)

    own_rows.wait()
    forward_rows(mine, chips - 1)
    for k, p in enumerate(peers):
        here = rows.at[:, p["x"], c, p["a"], p["b"]]
        pltpu.make_async_remote_copy(
            here, here, r_send.at[k], r_recv.at[chip_of(p)], device_id=sib, device_id_type=MESH
        ).wait_recv()
        forward_rows(p, k)
    for k, p in enumerate(peers + [mine]):
        here = rows.at[:, p["x"], 1 - c, p["a"], p["b"]]
        pltpu.make_async_remote_copy(
            here, here, f_send.at[k], f_recv.at[k], device_id=sib, device_id_type=MESH
        ).wait_recv()

    def result(strip, part):
        cols = pl.ds(pl.multiple_of(c * half + strip * STRIP, STRIP), STRIP)
        at = lax.rem(strip, 2)
        if part == 0:
            return pltpu.make_async_remote_copy(
                held.at[at, 0], hid_out.at[:, cols], o_send.at[at], o_recv.at[strip],
                device_id=sib, device_id_type=MESH,
            )
        return pltpu.make_async_copy(held.at[at, 1], hid_out.at[:, cols], o_own.at[at])

    def strip_step(strip, carry):
        @pl.when(strip >= 2)
        def _():
            result(strip - 2, 0).wait_send()
            result(strip - 2, 1).wait()

        cols = pl.ds(pl.multiple_of(strip * STRIP, STRIP), STRIP)
        for part in range(2):
            who = 1 - c if part == 0 else c
            mlp_in = rows[who].reshape(tok_dev, span_embed)
            g = jnp.dot(mlp_in, wide[0, :, cols], preferred_element_type=f32)
            u = jnp.dot(mlp_in, wide[1, :, cols], preferred_element_type=f32)
            held[lax.rem(strip, 2), part] = (g * jax.nn.sigmoid(g) * u).astype(bf16)
            result(strip, part).start()
        return carry

    for span, (start, width) in enumerate(spans):
        far(weights[span])
        lax.fori_loop(start // STRIP, (start + width) // STRIP, strip_step, 0)
    strips = half // STRIP
    for s in (strips - 2, strips - 1):
        result(jnp.int32(s), 0).wait_send()
        result(jnp.int32(s), 1).wait()
    for s in range(strips):
        result(jnp.int32(s), 0).wait_recv()
    res.wait()
    for d in sends:
        d.wait_send()


def layer(shape, slots, lens, tokens, wq, wk, wv, wo, shrink, grow, gate, up, gain1, gain2, want, source):
    X, A, B = shape
    chips = X * A * B
    tok_dev, depth = tokens.shape
    heads_wide = wq.shape[1]
    shard, width = gate.shape
    half = width // CORES
    block = tok_dev // (chips * CORES)
    spans = ((0, 768), (768, half - 768))
    n_items = 2 + 2 * len(spans)
    DMA = pltpu.SemaphoreType.DMA
    bf16 = jnp.bfloat16
    f32 = jnp.float32
    ANY = pl.BlockSpec(memory_space=pl.ANY)
    VM = pl.BlockSpec(memory_space=pltpu.VMEM)
    SM = pl.BlockSpec(memory_space=pltpu.SMEM)
    return pl.pallas_call(
        functools.partial(layer_kernel, shape, spans),
        out_shape=(
            jax.ShapeDtypeStruct((tok_dev, depth), bf16),
            jax.ShapeDtypeStruct((tok_dev, width), bf16),
        ),
        in_specs=[SM] * 2 + [ANY] * 9 + [VM] * 4,
        out_specs=(ANY, ANY),
        scratch_shapes=[
            pltpu.VMEM((tok_dev, depth), bf16),
            pltpu.VMEM((3, depth, heads_wide), bf16),
            pltpu.VMEM((heads_wide, depth), bf16),
            pltpu.VMEM((tok_dev, depth), bf16),
            pltpu.VMEM((tok_dev, heads_wide), f32),
            pltpu.VMEM((tok_dev, heads_wide), f32),
            pltpu.VMEM((tok_dev, heads_wide), bf16),
            pltpu.VMEM((tok_dev, heads_wide), bf16),
            pltpu.VMEM((tok_dev, heads_wide), bf16),
            pltpu.VMEM((tok_dev, heads_wide), bf16),
            pltpu.VMEM((tok_dev, depth), bf16),
            pltpu.VMEM((chips, CORES, block, depth), bf16),
            pltpu.VMEM((CORES, chips) + shrink.shape[1:], bf16),
            pltpu.VMEM((CORES, chips) + grow.shape[1:], bf16),
            pltpu.VMEM((2, CORES, shard, half), bf16),
            pltpu.VMEM((2, depth, half), bf16),
            pltpu.VMEM((CORES, X, CORES, A, B, block, depth), bf16),
            pltpu.VMEM((2, 2, tok_dev, STRIP), bf16),
            DMA((5,)), DMA((2,)), DMA((2,)), DMA((2,)), DMA((2,)),
            DMA((n_items * (chips - 1),)), DMA((n_items, chips)), DMA((2,)), DMA((2,)),
            DMA((chips,)), DMA((chips,)), DMA((chips,)), DMA((chips,)),
            DMA((2,)), DMA((2,)), DMA((half // STRIP,)), DMA((1,)),
        ],
        compiler_params=pltpu.CompilerParams(
            collective_id=0, has_side_effects=True, vmem_limit_bytes=62 << 20
        ),
        name="layer",
    )(slots, lens, tokens, wq, wk, wv, wo, shrink, grow, gate, up, gain1, gain2, want, source)


def local_fused(
    tokens, first_norm_gain, query_weight, key_weight, value_weight, output_weight, lengths,
    request_adapter, slot_adapter_ids, plugin_shrink_maps, plugin_grow_maps, device_token_order,
    second_norm_gain, gate_weight, up_weight,
):
    shape = tuple(lax.axis_size(n) for n in ("x", "a", "b"))
    mp = shape[1] * shape[2]
    chips = shape[0] * mp
    resident = plugin_shrink_maps.shape[0]
    tok_dev, depth = tokens.shape
    block = tok_dev // (chips * CORES)
    ids = jnp.arange(slot_adapter_ids.shape[0], dtype=jnp.int32)
    owner, within = ids // resident, ids % resident
    place = (within // CORES * mp + owner) * CORES + within % CORES
    match = slot_adapter_ids[None, :] == request_adapter[:, None]
    slots = jnp.sum(jnp.where(match, place[None, :], 0), axis=1)
    want = device_token_order.reshape(shape[0], CORES, mp, block).transpose(0, 2, 1, 3)
    shard = gate_weight.shape[0]
    source = np.arange(CORES * mp * shard).reshape(CORES, mp, shard).transpose(1, 0, 2)
    return layer(
        shape, slots, lengths, tokens, query_weight, key_weight, value_weight, output_weight,
        plugin_shrink_maps.transpose(0, 2, 1),
        plugin_grow_maps.reshape(resident, 2 * LATENT_BREADTH, -1),
        gate_weight, up_weight, first_norm_gain[None, :], second_norm_gain[None, :],
        want.reshape(-1, 1), jnp.asarray(source.reshape(1, -1), jnp.int32),
    )


def solution(mesh):
    dp, mp = mesh.devices.shape
    fast = 1
    while fast * fast * 4 <= mp:
        fast *= 2
    devices = dp * mp
    fits = (
        EMBED_SPAN // devices * CORES % 16 == 0
        and TOK_DEV // devices % 16 == 0
        and dp == APD
    )
    if fits:
        names = ("a", "b")
        fine = jax.sharding.Mesh(
            mesh.devices.reshape(dp // CORES, CORES, mp // fast, fast), ("x", "core", "a", "b")
        )
    else:
        names = ("mp",)
        fine = jax.sharding.Mesh(
            mesh.devices.reshape(dp // CORES, CORES, mp), ("x", "core", "mp")
        )
    rows = ("x", "core") + names
    return jax.shard_map(
        local_fused if fits else local_plain,
        mesh=fine,
        in_specs=(
            P(rows, None),
            P(),
            P(),
            P(),
            P(),
            P(),
            P(rows),
            P(rows),
            P(),
            P(names, None, None),
            P(names, None, None, None),
            P(rows, None),
            P(),
            P(rows, None),
            P(rows, None),
        ),
        out_specs=(P(rows, None), P(rows, None)),
        check_vma=False,
    )
```

```python
import functools

import jax
import jax.numpy as jnp
import numpy as np
from jax import lax
from jax.experimental import pallas as pl
from jax.experimental.pallas import tpu as pltpu
from jax.sharding import PartitionSpec as P

EMBED_SPAN = 1792
HEADS = 8
HD = 112
LATENT_BREADTH = 16
REQ_DEV = 8
TOK_DEV = 512
APD = 4
SLOTR = 64
WINDOW = 32
SINKS = 4


PLUGIN_STRENGTH = 2.0
EPSILON = 1e-05


def normalize(rows_in, gain_vec):
    floated = rows_in.astype(jnp.float32)
    scale = lax.rsqrt(jnp.mean(floated * floated, axis=-1, keepdims=True) + EPSILON)
    return (floated * scale * gain_vec).astype(jnp.bfloat16)


def attend(query, key, value, request_len):
    queries = query.reshape(REQ_DEV, SLOTR, HEADS, HD)
    head_keys = key.reshape(REQ_DEV, SLOTR, HEADS, HD)
    head_values = value.reshape(REQ_DEV, SLOTR, HEADS, HD)
    scores = jnp.einsum(
        "rqhd,rkhd->rhqk", queries, head_keys, preferred_element_type=jnp.float32
    ) * HD ** (-0.5)
    places = jnp.arange(SLOTR)
    query_place = places[:, None]
    key_place = places[None, :]
    allowed = (key_place <= query_place) & (
        (query_place - key_place < WINDOW) | (key_place < SINKS)
    )
    key_live = places[None, :] < request_len[:, None]
    visible_lookup_flags = allowed[None, None, :, :] & key_live[:, None, None, :]
    scores = jnp.where(visible_lookup_flags, scores, -1e30)
    row_max = jnp.max(scores, axis=-1, keepdims=True)
    expo = jnp.where(visible_lookup_flags, jnp.exp(scores - row_max), 0.0)
    softmax_w = (expo / jnp.sum(expo, axis=-1, keepdims=True)).astype(jnp.bfloat16)
    attended = jnp.einsum(
        "rhqk,rkhd->rqhd", softmax_w, head_values, preferred_element_type=jnp.float32
    ).astype(jnp.bfloat16)
    query_live = (places[None, :] < request_len[:, None])[:, :, None, None]
    attended = jnp.where(query_live, attended, jnp.zeros_like(attended))
    return attended.reshape(REQ_DEV * SLOTR, HEADS * HD)


CORES = 2


def gate_kernel(rows_ref, gain_ref, w_ref, act_ref, o_ref):
    @pl.when(pl.program_id(0) == 0)
    def _():
        @pl.loop(0, rows_ref.shape[0], step=64)
        def _(r):
            part = pl.ds(pl.multiple_of(r, 64), 64)
            wide = rows_ref[part, :].astype(jnp.float32)
            scale = lax.rsqrt(jnp.mean(wide * wide, axis=-1, keepdims=True) + EPSILON)
            act_ref[part, :] = (wide * scale * gain_ref[...]).astype(jnp.bfloat16)

    gate = jnp.dot(act_ref[...], w_ref[...], preferred_element_type=jnp.float32)
    o_ref[...] = gate * jax.nn.sigmoid(gate)


def gate_units(regrouped, gain, weight):
    rows, depth = regrouped.shape
    width = weight.shape[1]
    tile = 512
    whole = lambda i: (0, 0)
    strip = lambda i: (0, i)
    return pl.pallas_call(
        gate_kernel,
        out_shape=(
            jax.ShapeDtypeStruct((rows, depth), jnp.bfloat16),
            jax.ShapeDtypeStruct((rows, width), jnp.float32),
        ),
        grid=(width // tile,),
        in_specs=[
            pl.BlockSpec((rows, depth), whole),
            pl.BlockSpec((1, depth), whole),
            pl.BlockSpec((depth, tile), strip),
        ],
        out_specs=(pl.BlockSpec((rows, depth), whole), pl.BlockSpec((rows, tile), strip)),
        compiler_params=pltpu.CompilerParams(vmem_limit_bytes=32 << 20),
        name="gate_units",
    )(regrouped, gain[None, :], weight)


def up_kernel(act_ref, silu_ref, w_ref, o_ref):
    up = jnp.dot(act_ref[...], w_ref[...], preferred_element_type=jnp.float32)
    o_ref[...] = (silu_ref[...] * up).astype(o_ref.dtype)


def up_units(act, silu, weight):
    rows, depth = act.shape
    width = weight.shape[1]
    tile = 512
    strip = lambda i: (0, i)
    return pl.pallas_call(
        up_kernel,
        out_shape=jax.ShapeDtypeStruct((rows, width), jnp.bfloat16),
        grid=(width // tile,),
        in_specs=[
            pl.BlockSpec((rows, depth), lambda i: (0, 0)),
            pl.BlockSpec((rows, tile), strip),
            pl.BlockSpec((depth, tile), strip),
        ],
        out_specs=pl.BlockSpec((rows, tile), strip),
        compiler_params=pltpu.CompilerParams(vmem_limit_bytes=48 << 20),
        name="up_units",
    )(act, silu, weight)


def local_plain(
    tokens,
    first_norm_gain,
    query_weight,
    key_weight,
    value_weight,
    output_weight,
    lengths,
    request_adapter,
    slot_adapter_ids,
    plugin_shrink_maps,
    plugin_grow_maps,
    device_token_order,
    second_norm_gain,
    gate_weight,
    up_weight,
):
    owner_count = lax.axis_size("mp")
    resident_slots = plugin_shrink_maps.shape[0]
    tok_dev = tokens.shape[0]
    hw_size = query_weight.shape[1]
    every = ("x", "core", "mp")

    gate_full = lax.all_gather(gate_weight, every, axis=0, tiled=True)
    up_full = lax.all_gather(up_weight, every, axis=0, tiled=True)

    matches = (slot_adapter_ids[None, :] == request_adapter[:, None]).astype(jnp.int32)
    slot_ids = jnp.sum(
        matches * jnp.arange(slot_adapter_ids.shape[0], dtype=jnp.int32)[None, :], axis=1
    )
    owner_index = slot_ids // resident_slots
    within = slot_ids % resident_slots
    routing = (jnp.arange(owner_count)[:, None] == owner_index[None, :]).astype(jnp.bfloat16)
    slot_pick = (jnp.arange(resident_slots)[None, :] == within[:, None]).astype(jnp.bfloat16)
    chosen = jnp.dot(routing, slot_pick, preferred_element_type=jnp.float32).astype(jnp.bfloat16)
    chosen_adapter = lax.all_to_all(chosen, "mp", split_axis=0, concat_axis=0, tiled=True)
    maps = jnp.concatenate(
        [
            plugin_shrink_maps.transpose(0, 2, 1),
            plugin_grow_maps.reshape(resident_slots, 2 * LATENT_BREADTH, hw_size),
        ],
        axis=-1,
    )
    outgoing = jnp.einsum(
        "ge,ezc->gzc", chosen_adapter, maps, preferred_element_type=jnp.float32
    ).astype(jnp.bfloat16)
    incoming = lax.all_to_all(outgoing, "mp", split_axis=0, concat_axis=0, tiled=True)
    own_maps = jnp.einsum(
        "or,ozc->rzc", routing, incoming, preferred_element_type=jnp.float32
    ).astype(jnp.bfloat16)

    normed = normalize(tokens, first_norm_gain)
    request_rows = normed.reshape(REQ_DEV, SLOTR, EMBED_SPAN)
    codes = jnp.einsum(
        "rsd,rkd->rsk",
        request_rows,
        own_maps[..., :EMBED_SPAN],
        preferred_element_type=jnp.float32,
    ).astype(jnp.bfloat16)
    delta_q = (
        jnp.einsum(
            "rsk,rkh->rsh",
            codes[..., :LATENT_BREADTH],
            own_maps[:, :LATENT_BREADTH, EMBED_SPAN:],
            preferred_element_type=jnp.float32,
        )
        * PLUGIN_STRENGTH
    ).astype(jnp.bfloat16)
    delta_v = (
        jnp.einsum(
            "rsk,rkh->rsh",
            codes[..., LATENT_BREADTH:],
            own_maps[:, LATENT_BREADTH:, EMBED_SPAN:],
            preferred_element_type=jnp.float32,
        )
        * PLUGIN_STRENGTH
    ).astype(jnp.bfloat16)
    query = (
        jnp.dot(normed, query_weight, preferred_element_type=jnp.float32)
        + delta_q.reshape(tok_dev, hw_size).astype(jnp.float32)
    ).astype(jnp.bfloat16)
    key = jnp.dot(normed, key_weight, preferred_element_type=jnp.float32).astype(jnp.bfloat16)
    value = (
        jnp.dot(normed, value_weight, preferred_element_type=jnp.float32)
        + delta_v.reshape(tok_dev, hw_size).astype(jnp.float32)
    ).astype(jnp.bfloat16)
    attended = attend(query, key, value, lengths)
    residual = (
        tokens.astype(jnp.float32)
        + jnp.dot(attended, output_weight, preferred_element_type=jnp.float32)
    ).astype(jnp.bfloat16)
    order = device_token_order.reshape(-1, 1) == jnp.arange(tok_dev)[None, :]
    shuffled = jnp.dot(
        order.astype(jnp.bfloat16), residual, preferred_element_type=jnp.float32
    ).astype(jnp.bfloat16)
    regrouped = lax.all_to_all(shuffled, every, split_axis=0, concat_axis=0, tiled=True)
    act, silu = gate_units(regrouped, second_norm_gain, gate_full)
    hidden = up_units(act, silu, up_full)
    return (residual, hidden)


MESH = pl.DeviceIdType.MESH
STRIP = 256
PAIR = 2 * SLOTR
LANES = 128
NEVER = -1e30


def layer_kernel(
    shape, spans,
    lens, chosen, stored, tokens, wq, wk, wv, wo, shrink, grow, gate, up, gain1, gain2, want, source,
    res_out, hid_out,
    tok, wqkv, wout, normed, qf, vf, kb, qb, vb, att, act, shuf,
    ads, adg, stage, wide, rows, held,
    load_sem, ad_sem, swap_send, swap_recv, swap_own, i_send, i_recv, m_send, m_recv,
    r_send, r_recv, f_send, f_recv, o_own, o_send, o_recv, res_sem,
):
    X, A, B = shape
    x, c, a, b = (lax.axis_index(n) for n in ("x", "core", "a", "b"))
    sib = {"core": 1 - c}
    sizes = {"x": X, "a": A, "b": B}
    mine = {"x": x, "a": a, "b": b}
    depth = gate.shape[0]
    half = wide.shape[2]
    chips = X * A * B
    tok_dev = tok.shape[0]
    span_embed = tok.shape[1]
    heads_wide = kb.shape[1]
    f32 = jnp.float32
    bf16 = jnp.bfloat16

    def chip_of(at):
        return (at["x"] * A + at["a"]) * B + at["b"]

    def moved(at, axis, k):
        return {**at, axis: lax.rem(at[axis] + k, sizes[axis])}

    me = chip_of(mine)
    which = x * CORES + c
    loads = []
    own_ads = []
    for k, (frm, to) in enumerate(((shrink, ads), (grow, adg))):
        d = pltpu.make_async_copy(frm.at[which], to.at[c, me], ad_sem.at[k])
        d.start()
        own_ads.append(d)
    for k, (frm, to) in enumerate(
        ((tokens, tok), (wk, wqkv.at[1]), (wq, wqkv.at[0]), (wv, wqkv.at[2]), (wo, wout))
    ):
        d = pltpu.make_async_copy(frm, to, load_sem.at[k])
        d.start()
        loads.append(d)
    theirs = pl.ds(pl.multiple_of((1 - c) * half, half), half)
    ours = pl.ds(pl.multiple_of(c * half, half), half)
    own_halves = []
    for mat, w in enumerate((gate, up)):
        d = pltpu.make_async_copy(w.at[:, ours], stage.at[mat, c], swap_own.at[mat])
        d.start()
        own_halves.append(d)

    barrier = pltpu.get_barrier_semaphore()
    peers = []
    for i in range(X):
        for j in range(A):
            for k in range(B):
                if i or j or k:
                    peers.append(moved(moved(moved(mine, "x", i), "a", j), "b", k))
    pl.semaphore_signal(barrier, inc=1, device_id=sib, device_id_type=MESH)
    for p in peers:
        pl.semaphore_signal(barrier, inc=1, device_id=p, device_id_type=MESH)
    pl.semaphore_wait(barrier, chips)

    sends = []
    swaps = []
    for mat, w in enumerate((gate, up)):
        s = pltpu.make_async_remote_copy(
            w.at[:, theirs], stage.at[mat, c], swap_send.at[mat], swap_recv.at[mat],
            device_id=sib, device_id_type=MESH,
        )
        s.start()
        swaps.append(s)

    def weight_slot(mat, span):
        start, width = spans[span]

        def get(chip):
            at = pl.ds(pl.multiple_of(chip * 2 * depth, 16), 2 * depth)
            return wide.at[mat, at, pl.ds(start, width)]

        return get

    items = [
        (lambda chip: ads.at[c, chip], ("a", "b", "x")),
        (lambda chip: adg.at[c, chip], ("a", "x", "b")),
    ]
    ADAPT = (0, 1)
    orders = ((("a", "x", "b"), ("a", "b", "x")),) * 2
    weights = []
    for span in range(len(spans)):
        weights.append((len(items), len(items) + 1))
        for mat in range(2):
            items.append((weight_slot(mat, span), orders[span][mat]))

    line = (
        a,
        a + 1 - 2 * lax.rem(a, 2),
        jnp.where(a < A // 2, 2, 1),
        jnp.where(a < A // 2, A - 1, 0),
    )
    onward = tuple(2 * a - s if n == 1 else jnp.where(s < a, a + 1, a - 1) for n, s in enumerate(line))
    all_at = [
        {"x": i, "a": j, "b": k} for i in range(X) for j in range(A) for k in range(B)
    ]

    def place_of(rel):
        return {
            "x": lax.rem(x + rel["x"], X), "a": line[rel["a"]], "b": lax.rem(b + rel["b"], B)
        }

    def hops(rel):
        return rel["x"] + rel["a"] + rel["b"]

    count = [0]

    def push(n, chip, to, when):
        ref = items[n][0](chip)
        d = pltpu.make_async_remote_copy(
            ref, ref, i_send.at[count[0]], i_recv.at[n, chip], device_id=to, device_id_type=MESH
        )
        count[0] += 1
        sends.append((d, when))
        if when is None:
            d.start()
        else:
            pl.when(when)(d.start)

    def spread(n, rel):
        order = items[n][1]
        last = max([order.index(k) for k in order if rel[k]], default=-1)
        chip = chip_of(place_of(rel))
        for axis in order[max(last, 0):]:
            if axis == "a":
                if rel["a"] == 0:
                    push(n, chip, {"a": jnp.minimum(a + 1, A - 1)}, a + 1 < A)
                    push(n, chip, {"a": jnp.maximum(a - 1, 0)}, a > 0)
                else:
                    to = onward[rel["a"]]
                    push(n, chip, {"a": jnp.clip(to, 0, A - 1)}, (to >= 0) & (to < A))
            elif rel[axis] == 0:
                push(n, chip, {axis: 1 - mine[axis]}, None)

    def arrived(n, rel):
        chip = chip_of(place_of(rel))
        ref = items[n][0](chip)
        pltpu.make_async_remote_copy(
            ref, ref, i_send.at[0], i_recv.at[n, chip], device_id=sib, device_id_type=MESH
        ).wait_recv()

    def passes(n, rel):
        return hops(rel) > 0 and rel[items[n][1][2]] == 0

    def begin(ns):
        for n in ns:
            spread(n, all_at[0])

    def stage_of(ns, h):
        for n in ns:
            for rel in all_at:
                if hops(rel) == h and passes(n, rel):
                    arrived(n, rel)
                    spread(n, rel)

    def finish(ns):
        for n in ns:
            for rel in all_at:
                if hops(rel) and not passes(n, rel):
                    arrived(n, rel)

    for d in own_ads:
        d.wait()
    begin(ADAPT)

    def join_halves():
        for mat in range(2):
            own_halves[mat].wait()
            swaps[mat].wait()
            joined = jnp.concatenate(
                [stage[mat, 0].astype(f32), stage[mat, 1].astype(f32)], axis=0
            ).astype(bf16)
            wide[mat, pl.ds(pl.multiple_of(me * 2 * depth, 16), 2 * depth), :] = joined
    def norm_rows():
        loads[0].wait()

        @pl.loop(0, tok_dev, step=PAIR)
        def _(r):
            part = pl.ds(pl.multiple_of(r, PAIR), PAIR)
            wf = tok[part, :].astype(f32)
            scale = lax.rsqrt(jnp.mean(wf * wf, axis=-1, keepdims=True) + EPSILON)
            normed[part, :] = (wf * scale * gain1[...].reshape(1, span_embed)).astype(bf16)

    def project(k, to):
        loads[(2, 1, 3)[k]].wait()

        @pl.loop(0, tok_dev, step=256)
        def _(r):
            part = pl.ds(pl.multiple_of(r, 256), 256)
            to[part, :] = jnp.dot(
                normed[part, :], wqkv[k], preferred_element_type=f32
            ).astype(to.dtype)

    shares = []

    def share():
        finish(ADAPT)
        for k, ref in enumerate((ads, adg)):
            d = pltpu.make_async_remote_copy(
                ref.at[c], ref.at[c], m_send.at[k], m_recv.at[k],
                device_id=sib, device_id_type=MESH,
            )
            d.start()
            shares.append(d)

    def shared():
        for d in shares:
            d.wait()

    column = lax.broadcasted_iota(jnp.int32, (1, heads_wide), 1)

    def pair_step(pair, carry):
        for n in range(2):
            r = pair * 2 + n
            part = pl.ds(pl.multiple_of(r * SLOTR, SLOTR), SLOTR)
            slot = lax.fori_loop(
                0, stored.shape[0], lambda s, got: jnp.where(stored[s] == chosen[r], s, got), 0
            )
            core_at = slot % CORES
            chip_at = slot % (X * CORES) // CORES * (A * B) + slot // (X * CORES)
            codes = lax.dot_general(
                normed[part, :], ads[core_at, chip_at],
                (((1,), (1,)), ((), ())), preferred_element_type=f32,
            ).astype(bf16)
            g = adg[core_at, chip_at]
            lane = lax.broadcasted_iota(jnp.int32, codes.shape, 1)
            none = jnp.zeros_like(codes)
            for low, base, to in ((True, qf, qb), (False, vf, vb)):
                kept = jnp.where((lane < LATENT_BREADTH) == low, codes, none)
                delta = jnp.dot(kept, g, preferred_element_type=f32) * PLUGIN_STRENGTH
                to[part, :] = (base[part, :] + delta.astype(bf16).astype(f32)).astype(bf16)
        part = pl.ds(pl.multiple_of(pair * PAIR, PAIR), PAIR)
        i = lax.broadcasted_iota(jnp.int32, (PAIR, PAIR), 0)
        j = lax.broadcasted_iota(jnp.int32, (PAIR, PAIR), 1)
        len0, len1 = lens[pair * 2], lens[pair * 2 + 1]
        qi = jnp.where(i < SLOTR, i, i - SLOTR)
        kj = jnp.where(j < SLOTR, j, j - SLOTR)
        same = (i < SLOTR) == (j < SLOTR)
        live = kj < jnp.where(j < SLOTR, len0, len1)
        seen = same & live & (kj <= qi) & ((qi - kj < WINDOW) | (kj < SINKS))
        row = lax.broadcasted_iota(jnp.int32, (PAIR, 1), 0)
        alive = jnp.where(row < SLOTR, row, row - SLOTR) < jnp.where(row < SLOTR, len0, len1)
        before = None
        for h in range(HEADS):
            lo, hi = h * HD, (h + 1) * HD
            first, last = lo // LANES, (hi - 1) // LANES
            cols = slice(first * LANES, (last + 1) * LANES)
            q = qb[part, cols]
            pick = (column[:, cols] >= lo) & (column[:, cols] < hi)
            q = jnp.where(pick, q, jnp.zeros_like(q))
            s = lax.dot_general(
                q, kb[part, cols], (((1,), (1,)), ((), ())), preferred_element_type=f32
            ) * HD ** (-0.5)
            s = jnp.where(seen, s, NEVER)
            e = jnp.where(seen, jnp.exp(s - jnp.max(s, axis=-1, keepdims=True)), 0.0)
            p = (e / jnp.sum(e, axis=-1, keepdims=True)).astype(bf16)
            o = jnp.dot(p, vb[part, cols], preferred_element_type=f32)
            o = jnp.where(alive, o, 0.0).astype(bf16)
            if h > 0:
                w = h - 1
                at = column[:, w * LANES:(w + 1) * LANES]
                att[part, w * LANES:(w + 1) * LANES] = jnp.where(at < lo, before, o[:, :LANES])
            before = o[:, -LANES:]
        return carry

    def attend_pairs(first, last):
        lax.fori_loop(first, last, pair_step, 0)

    group = source.shape[1]
    ahead = lax.broadcasted_iota(jnp.int32, (group, group), 0)
    turn = jnp.where(ahead == source[...], 1.0, 0.0).astype(bf16)

    def project_out():
        loads[4].wait()

        @pl.loop(0, tok_dev, step=PAIR)
        def _(r):
            part = pl.ds(pl.multiple_of(r, PAIR), PAIR)
            mixed = tok[part, :].astype(f32) + jnp.dot(
                att[part, :], wout[...], preferred_element_type=f32
            )
            mixed = mixed.astype(bf16)
            tok[part, :] = mixed
            wf = mixed.astype(f32)
            scale = lax.rsqrt(jnp.mean(wf * wf, axis=-1, keepdims=True) + EPSILON)
            nb = (wf * scale * gain2[...].reshape(1, span_embed)).astype(bf16)
            for g in range(span_embed // group):
                cols = slice(g * group, (g + 1) * group)
                act[part, cols] = jnp.dot(nb[:, cols], turn, preferred_element_type=f32).astype(bf16)

    res = pltpu.make_async_copy(tok, res_out, res_sem.at[0])
    own_rows = pltpu.make_async_copy(shuf.at[x, :, a, b], rows.at[:, x, c, a, b], r_recv.at[me])
    block = rows.shape[5]
    def regroup():
        res.start()
        size = A * B * block
        for i in range(X):
            for k in range(CORES):
                n = i * CORES + k
                rank = lax.broadcasted_iota(jnp.int32, (tok_dev, size), 0)
                one = jnp.where(rank == want[:, n * size:(n + 1) * size], 1.0, 0.0).astype(bf16)
                ordered = lax.dot_general(
                    one, act[...], (((0,), (0,)), ((), ())), preferred_element_type=f32
                ).astype(bf16)
                shuf[i, k] = ordered.reshape(A, B, block, span_embed)

        for k, p in enumerate(peers):
            d = pltpu.make_async_remote_copy(
                shuf.at[p["x"], :, p["a"], p["b"]], rows.at[:, x, c, a, b], r_send.at[k], r_recv.at[me],
                device_id=p, device_id_type=MESH,
            )
            d.start()
            sends.append((d, None))
        own_rows.start()

    def forward_rows(p, k):
        here = rows.at[:, p["x"], c, p["a"], p["b"]]
        d = pltpu.make_async_remote_copy(
            here, here, f_send.at[k], f_recv.at[k], device_id=sib, device_id_type=MESH
        )
        d.start()
        sends.append((d, None))

    def share_rows():
        own_rows.wait()
        forward_rows(mine, chips - 1)
        for k, p in enumerate(peers):
            here = rows.at[:, p["x"], c, p["a"], p["b"]]
            pltpu.make_async_remote_copy(
                here, here, r_send.at[k], r_recv.at[chip_of(p)], device_id=sib, device_id_type=MESH
            ).wait_recv()
            forward_rows(p, k)

    def rows_shared():
        for k, p in enumerate(peers + [mine]):
            here = rows.at[:, p["x"], 1 - c, p["a"], p["b"]]
            pltpu.make_async_remote_copy(
                here, here, f_send.at[k], f_recv.at[k], device_id=sib, device_id_type=MESH
            ).wait_recv()

    def result(strip, part):
        cols = pl.ds(pl.multiple_of(c * half + strip * STRIP, STRIP), STRIP)
        at = lax.rem(strip, 2)
        if part == 0:
            return pltpu.make_async_remote_copy(
                held.at[at, 0], hid_out.at[:, cols], o_send.at[at], o_recv.at[strip],
                device_id=sib, device_id_type=MESH,
            )
        return pltpu.make_async_copy(held.at[at, 1], hid_out.at[:, cols], o_own.at[at])

    def strip_step(strip, carry):
        @pl.when(strip >= 2)
        def _():
            result(strip - 2, 0).wait_send()
            result(strip - 2, 1).wait()

        cols = pl.ds(pl.multiple_of(strip * STRIP, STRIP), STRIP)
        for part in range(2):
            who = 1 - c if part == 0 else c
            mlp_in = rows[who].reshape(tok_dev, span_embed)
            g = jnp.dot(mlp_in, wide[0, :, cols], preferred_element_type=f32)
            u = jnp.dot(mlp_in, wide[1, :, cols], preferred_element_type=f32)
            held[lax.rem(strip, 2), part] = (g * jax.nn.sigmoid(g) * u).astype(bf16)
            result(strip, part).start()
        return carry

    def hidden_units(span):
        start, width = spans[span]
        finish(weights[span])
        lax.fori_loop(start // STRIP, (start + width) // STRIP, strip_step, 0)

    join_halves()
    norm_rows()
    stage_of(ADAPT, 1)
    begin(weights[1])
    begin(weights[0])
    project(1, kb)
    stage_of(ADAPT, 2)
    stage_of(weights[1], 1)
    stage_of(weights[0], 1)
    project(0, qf)
    stage_of(ADAPT, 3)
    stage_of(ADAPT, 4)
    project(2, vf)
    share()
    stage_of(weights[1], 2)
    stage_of(weights[0], 2)
    shared()
    attend_pairs(0, 1)
    attend_pairs(1, 2)
    stage_of(weights[1], 3)
    attend_pairs(2, 3)
    attend_pairs(3, 4)
    stage_of(weights[0], 3)
    project_out()
    regroup()
    stage_of(weights[0], 4)
    stage_of(weights[1], 4)
    share_rows()
    rows_shared()
    hidden_units(0)
    hidden_units(1)

    strips = half // STRIP
    for s in (strips - 2, strips - 1):
        result(jnp.int32(s), 0).wait_send()
        result(jnp.int32(s), 1).wait()
    for s in range(strips):
        result(jnp.int32(s), 0).wait_recv()
    res.wait()
    for d, when in sends:
        if when is None:
            d.wait_send()
        else:
            pl.when(when)(d.wait_send)


def layer(shape, lens, chosen, stored, tokens, wq, wk, wv, wo, shrink, grow, gate, up, gain1, gain2, want, source):
    X, A, B = shape
    chips = X * A * B
    tok_dev, depth = tokens.shape
    heads_wide = wq.shape[1]
    shard, width = gate.shape
    half = width // CORES
    block = tok_dev // (chips * CORES)
    spans = ((0, 768), (768, half - 768))
    n_items = 2 + 2 * len(spans)
    DMA = pltpu.SemaphoreType.DMA
    bf16 = jnp.bfloat16
    f32 = jnp.float32
    ANY = pl.BlockSpec(memory_space=pl.ANY)
    VM = pl.BlockSpec(memory_space=pltpu.VMEM)
    SM = pl.BlockSpec(memory_space=pltpu.SMEM)
    return pl.pallas_call(
        functools.partial(layer_kernel, shape, spans),
        out_shape=(
            jax.ShapeDtypeStruct((tok_dev, depth), bf16),
            jax.ShapeDtypeStruct((tok_dev, width), bf16),
        ),
        in_specs=[SM] * 3 + [ANY] * 9 + [VM] * 4,
        out_specs=(ANY, ANY),
        scratch_shapes=[
            pltpu.VMEM((tok_dev, depth), bf16),
            pltpu.VMEM((3, depth, heads_wide), bf16),
            pltpu.VMEM((heads_wide, depth), bf16),
            pltpu.VMEM((tok_dev, depth), bf16),
            pltpu.VMEM((tok_dev, heads_wide), f32),
            pltpu.VMEM((tok_dev, heads_wide), f32),
            pltpu.VMEM((tok_dev, heads_wide), bf16),
            pltpu.VMEM((tok_dev, heads_wide), bf16),
            pltpu.VMEM((tok_dev, heads_wide), bf16),
            pltpu.VMEM((tok_dev, heads_wide), bf16),
            pltpu.VMEM((tok_dev, depth), bf16),
            pltpu.VMEM((X, CORES, A, B, block, depth), bf16),
            pltpu.VMEM((CORES, chips) + shrink.shape[1:], bf16),
            pltpu.VMEM((CORES, chips) + grow.shape[1:], bf16),
            pltpu.VMEM((2, CORES, shard, half), bf16),
            pltpu.VMEM((2, depth, half), bf16),
            pltpu.VMEM((CORES, X, CORES, A, B, block, depth), bf16),
            pltpu.VMEM((2, 2, tok_dev, STRIP), bf16),
            DMA((5,)), DMA((2,)), DMA((2,)), DMA((2,)), DMA((2,)),
            DMA((n_items * 2 * chips,)), DMA((n_items, chips)), DMA((2,)), DMA((2,)),
            DMA((chips,)), DMA((chips,)), DMA((chips,)), DMA((chips,)),
            DMA((2,)), DMA((2,)), DMA((half // STRIP,)), DMA((1,)),
        ],
        compiler_params=pltpu.CompilerParams(
            collective_id=0, has_side_effects=True, vmem_limit_bytes=62 << 20
        ),
        name="layer",
    )(lens, chosen, stored, tokens, wq, wk, wv, wo, shrink, grow, gate, up, gain1, gain2, want, source)


def local_fused(
    tokens, first_norm_gain, query_weight, key_weight, value_weight, output_weight, lengths,
    request_adapter, slot_adapter_ids, plugin_shrink_maps, plugin_grow_maps, device_token_order,
    second_norm_gain, gate_weight, up_weight,
):
    shape = tuple(lax.axis_size(n) for n in ("x", "a", "b"))
    mp = shape[1] * shape[2]
    resident = plugin_shrink_maps.shape[0]
    shard = gate_weight.shape[0]
    source = np.arange(CORES * mp * shard).reshape(CORES, mp, shard).transpose(1, 0, 2)
    return layer(
        shape, lengths, request_adapter, slot_adapter_ids, tokens, query_weight, key_weight, value_weight, output_weight,
        plugin_shrink_maps.transpose(0, 2, 1),
        plugin_grow_maps.reshape(resident, 2 * LATENT_BREADTH, -1),
        gate_weight, up_weight, first_norm_gain, second_norm_gain,
        device_token_order, jnp.asarray(source.reshape(1, -1), jnp.int32),
    )


def solution(mesh):
    dp, mp = mesh.devices.shape
    fast = 1
    while fast * fast * 4 <= mp:
        fast *= 2
    devices = dp * mp
    fits = (
        EMBED_SPAN // devices * CORES % 16 == 0
        and TOK_DEV // devices % 16 == 0
        and dp == APD
        and mp == 2 * APD
    )
    if fits:
        names = ("a", "b")
        fine = jax.sharding.Mesh(
            mesh.devices.reshape(dp // CORES, CORES, mp // fast, fast), ("x", "core", "a", "b")
        )
    else:
        names = ("mp",)
        fine = jax.sharding.Mesh(
            mesh.devices.reshape(dp // CORES, CORES, mp), ("x", "core", "mp")
        )
    rows = ("x", "core") + names
    return jax.shard_map(
        local_fused if fits else local_plain,
        mesh=fine,
        in_specs=(
            P(rows, None),
            P(),
            P(),
            P(),
            P(),
            P(),
            P(rows),
            P(rows),
            P(),
            P(names, None, None),
            P(names, None, None, None),
            P(rows, None),
            P(),
            P(rows, None),
            P(rows, None),
        ),
        out_specs=(P(rows, None), P(rows, None)),
        check_vma=False,
    )
```

```python
import functools

import jax
import jax.numpy as jnp
import numpy as np
from jax import lax
from jax.experimental import pallas as pl
from jax.experimental.pallas import tpu as pltpu
from jax.sharding import PartitionSpec as P

EMBED_SPAN = 1792
HEADS = 8
HD = 112
LATENT_BREADTH = 16
REQ_DEV = 8
TOK_DEV = 512
APD = 4
SLOTR = 64
WINDOW = 32
SINKS = 4


PLUGIN_STRENGTH = 2.0
EPSILON = 1e-05


def normalize(rows_in, gain_vec):
    floated = rows_in.astype(jnp.float32)
    scale = lax.rsqrt(jnp.mean(floated * floated, axis=-1, keepdims=True) + EPSILON)
    return (floated * scale * gain_vec).astype(jnp.bfloat16)


def attend(query, key, value, request_len):
    queries = query.reshape(REQ_DEV, SLOTR, HEADS, HD)
    head_keys = key.reshape(REQ_DEV, SLOTR, HEADS, HD)
    head_values = value.reshape(REQ_DEV, SLOTR, HEADS, HD)
    scores = jnp.einsum(
        "rqhd,rkhd->rhqk", queries, head_keys, preferred_element_type=jnp.float32
    ) * HD ** (-0.5)
    places = jnp.arange(SLOTR)
    query_place = places[:, None]
    key_place = places[None, :]
    allowed = (key_place <= query_place) & (
        (query_place - key_place < WINDOW) | (key_place < SINKS)
    )
    key_live = places[None, :] < request_len[:, None]
    visible_lookup_flags = allowed[None, None, :, :] & key_live[:, None, None, :]
    scores = jnp.where(visible_lookup_flags, scores, -1e30)
    row_max = jnp.max(scores, axis=-1, keepdims=True)
    expo = jnp.where(visible_lookup_flags, jnp.exp(scores - row_max), 0.0)
    softmax_w = (expo / jnp.sum(expo, axis=-1, keepdims=True)).astype(jnp.bfloat16)
    attended = jnp.einsum(
        "rhqk,rkhd->rqhd", softmax_w, head_values, preferred_element_type=jnp.float32
    ).astype(jnp.bfloat16)
    query_live = (places[None, :] < request_len[:, None])[:, :, None, None]
    attended = jnp.where(query_live, attended, jnp.zeros_like(attended))
    return attended.reshape(REQ_DEV * SLOTR, HEADS * HD)


CORES = 2


def gate_kernel(rows_ref, gain_ref, w_ref, act_ref, o_ref):
    @pl.when(pl.program_id(0) == 0)
    def _():
        @pl.loop(0, rows_ref.shape[0], step=64)
        def _(r):
            part = pl.ds(pl.multiple_of(r, 64), 64)
            wide = rows_ref[part, :].astype(jnp.float32)
            scale = lax.rsqrt(jnp.mean(wide * wide, axis=-1, keepdims=True) + EPSILON)
            act_ref[part, :] = (wide * scale * gain_ref[...]).astype(jnp.bfloat16)

    gate = jnp.dot(act_ref[...], w_ref[...], preferred_element_type=jnp.float32)
    o_ref[...] = gate * jax.nn.sigmoid(gate)


def gate_units(regrouped, gain, weight):
    rows, depth = regrouped.shape
    width = weight.shape[1]
    tile = 512
    whole = lambda i: (0, 0)
    strip = lambda i: (0, i)
    return pl.pallas_call(
        gate_kernel,
        out_shape=(
            jax.ShapeDtypeStruct((rows, depth), jnp.bfloat16),
            jax.ShapeDtypeStruct((rows, width), jnp.float32),
        ),
        grid=(width // tile,),
        in_specs=[
            pl.BlockSpec((rows, depth), whole),
            pl.BlockSpec((1, depth), whole),
            pl.BlockSpec((depth, tile), strip),
        ],
        out_specs=(pl.BlockSpec((rows, depth), whole), pl.BlockSpec((rows, tile), strip)),
        compiler_params=pltpu.CompilerParams(vmem_limit_bytes=32 << 20),
        name="gate_units",
    )(regrouped, gain[None, :], weight)


def up_kernel(act_ref, silu_ref, w_ref, o_ref):
    up = jnp.dot(act_ref[...], w_ref[...], preferred_element_type=jnp.float32)
    o_ref[...] = (silu_ref[...] * up).astype(o_ref.dtype)


def up_units(act, silu, weight):
    rows, depth = act.shape
    width = weight.shape[1]
    tile = 512
    strip = lambda i: (0, i)
    return pl.pallas_call(
        up_kernel,
        out_shape=jax.ShapeDtypeStruct((rows, width), jnp.bfloat16),
        grid=(width // tile,),
        in_specs=[
            pl.BlockSpec((rows, depth), lambda i: (0, 0)),
            pl.BlockSpec((rows, tile), strip),
            pl.BlockSpec((depth, tile), strip),
        ],
        out_specs=pl.BlockSpec((rows, tile), strip),
        compiler_params=pltpu.CompilerParams(vmem_limit_bytes=48 << 20),
        name="up_units",
    )(act, silu, weight)


def local_plain(
    tokens,
    first_norm_gain,
    query_weight,
    key_weight,
    value_weight,
    output_weight,
    lengths,
    request_adapter,
    slot_adapter_ids,
    plugin_shrink_maps,
    plugin_grow_maps,
    device_token_order,
    second_norm_gain,
    gate_weight,
    up_weight,
):
    owner_count = lax.axis_size("mp")
    resident_slots = plugin_shrink_maps.shape[0]
    tok_dev = tokens.shape[0]
    hw_size = query_weight.shape[1]
    every = ("x", "core", "mp")

    gate_full = lax.all_gather(gate_weight, every, axis=0, tiled=True)
    up_full = lax.all_gather(up_weight, every, axis=0, tiled=True)

    matches = (slot_adapter_ids[None, :] == request_adapter[:, None]).astype(jnp.int32)
    slot_ids = jnp.sum(
        matches * jnp.arange(slot_adapter_ids.shape[0], dtype=jnp.int32)[None, :], axis=1
    )
    owner_index = slot_ids // resident_slots
    within = slot_ids % resident_slots
    routing = (jnp.arange(owner_count)[:, None] == owner_index[None, :]).astype(jnp.bfloat16)
    slot_pick = (jnp.arange(resident_slots)[None, :] == within[:, None]).astype(jnp.bfloat16)
    chosen = jnp.dot(routing, slot_pick, preferred_element_type=jnp.float32).astype(jnp.bfloat16)
    chosen_adapter = lax.all_to_all(chosen, "mp", split_axis=0, concat_axis=0, tiled=True)
    maps = jnp.concatenate(
        [
            plugin_shrink_maps.transpose(0, 2, 1),
            plugin_grow_maps.reshape(resident_slots, 2 * LATENT_BREADTH, hw_size),
        ],
        axis=-1,
    )
    outgoing = jnp.einsum(
        "ge,ezc->gzc", chosen_adapter, maps, preferred_element_type=jnp.float32
    ).astype(jnp.bfloat16)
    incoming = lax.all_to_all(outgoing, "mp", split_axis=0, concat_axis=0, tiled=True)
    own_maps = jnp.einsum(
        "or,ozc->rzc", routing, incoming, preferred_element_type=jnp.float32
    ).astype(jnp.bfloat16)

    normed = normalize(tokens, first_norm_gain)
    request_rows = normed.reshape(REQ_DEV, SLOTR, EMBED_SPAN)
    codes = jnp.einsum(
        "rsd,rkd->rsk",
        request_rows,
        own_maps[..., :EMBED_SPAN],
        preferred_element_type=jnp.float32,
    ).astype(jnp.bfloat16)
    delta_q = (
        jnp.einsum(
            "rsk,rkh->rsh",
            codes[..., :LATENT_BREADTH],
            own_maps[:, :LATENT_BREADTH, EMBED_SPAN:],
            preferred_element_type=jnp.float32,
        )
        * PLUGIN_STRENGTH
    ).astype(jnp.bfloat16)
    delta_v = (
        jnp.einsum(
            "rsk,rkh->rsh",
            codes[..., LATENT_BREADTH:],
            own_maps[:, LATENT_BREADTH:, EMBED_SPAN:],
            preferred_element_type=jnp.float32,
        )
        * PLUGIN_STRENGTH
    ).astype(jnp.bfloat16)
    query = (
        jnp.dot(normed, query_weight, preferred_element_type=jnp.float32)
        + delta_q.reshape(tok_dev, hw_size).astype(jnp.float32)
    ).astype(jnp.bfloat16)
    key = jnp.dot(normed, key_weight, preferred_element_type=jnp.float32).astype(jnp.bfloat16)
    value = (
        jnp.dot(normed, value_weight, preferred_element_type=jnp.float32)
        + delta_v.reshape(tok_dev, hw_size).astype(jnp.float32)
    ).astype(jnp.bfloat16)
    attended = attend(query, key, value, lengths)
    residual = (
        tokens.astype(jnp.float32)
        + jnp.dot(attended, output_weight, preferred_element_type=jnp.float32)
    ).astype(jnp.bfloat16)
    order = device_token_order.reshape(-1, 1) == jnp.arange(tok_dev)[None, :]
    shuffled = jnp.dot(
        order.astype(jnp.bfloat16), residual, preferred_element_type=jnp.float32
    ).astype(jnp.bfloat16)
    regrouped = lax.all_to_all(shuffled, every, split_axis=0, concat_axis=0, tiled=True)
    act, silu = gate_units(regrouped, second_norm_gain, gate_full)
    hidden = up_units(act, silu, up_full)
    return (residual, hidden)


MESH = pl.DeviceIdType.MESH
STRIP = 256
PAIR = 2 * SLOTR
LANES = 128
NEVER = -1e30


def layer_kernel(
    shape, spans,
    lens, chosen, stored, tokens, wq, wk, wv, wo, shrink, grow, gate, up, gain1, gain2, want, source,
    res_out, hid_out,
    tok, wqkv, wout, normed, qf, vf, kb, qb, vb, att, act, shuf,
    slot_of, maps, picks, asked, chosen_out, chosen_in, stage, wide, rows, held,
    load_sem, ad_sem, swap_send, swap_recv, swap_own, i_send, i_recv, q_send, q_recv, m_send, m_recv,
    r_send, r_recv, f_send, f_recv, o_own, o_send, o_recv, res_sem,
):
    X, A, B = shape
    x, c, a, b = (lax.axis_index(n) for n in ("x", "core", "a", "b"))
    sib = {"core": 1 - c}
    sizes = {"x": X, "a": A, "b": B}
    mine = {"x": x, "a": a, "b": b}
    depth = gate.shape[0]
    half = wide.shape[2]
    chips = X * A * B
    tok_dev = tok.shape[0]
    span_embed = tok.shape[1]
    heads_wide = kb.shape[1]
    f32 = jnp.float32
    bf16 = jnp.bfloat16

    def chip_of(at):
        return (at["x"] * A + at["a"]) * B + at["b"]

    def moved(at, axis, k):
        return {**at, axis: lax.rem(at[axis] + k, sizes[axis])}

    me = chip_of(mine)
    group_size = A * B
    my_mp = a * B + b
    embed = shrink.shape[2]
    loads = []
    own_ads = []
    for k, (frm, to) in enumerate(
        ((shrink, maps.at[:, :, :embed]), (grow, maps.at[:, :, embed:]))
    ):
        d = pltpu.make_async_copy(frm, to, ad_sem.at[k])
        d.start()
        own_ads.append(d)
    for k, (frm, to) in enumerate(
        ((tokens, tok), (wk, wqkv.at[1]), (wq, wqkv.at[0]), (wv, wqkv.at[2]), (wo, wout))
    ):
        d = pltpu.make_async_copy(frm, to, load_sem.at[k])
        d.start()
        loads.append(d)
    theirs = pl.ds(pl.multiple_of((1 - c) * half, half), half)
    ours = pl.ds(pl.multiple_of(c * half, half), half)
    own_halves = []
    for mat, w in enumerate((gate, up)):
        d = pltpu.make_async_copy(w.at[:, ours], stage.at[mat, c], swap_own.at[mat])
        d.start()
        own_halves.append(d)

    count_req = chosen.shape[0]

    def look(s, got):
        here = stored[s]
        return tuple(jnp.where(here == chosen[r], s, g) for r, g in enumerate(got))

    found = lax.fori_loop(0, stored.shape[0], look, (jnp.int32(0),) * count_req)
    for r, s in enumerate(found):
        slot_of[r] = s
    for m in range(group_size):
        ask = jnp.int32(0)
        for s in found:
            ask = jnp.where(s // maps.shape[0] == m, s % maps.shape[0], ask)
        picks[m] = jnp.full(picks.shape[1:], ask, jnp.int32)

    barrier = pltpu.get_barrier_semaphore()
    peers = []
    for i in range(X):
        for j in range(A):
            for k in range(B):
                if i or j or k:
                    peers.append(moved(moved(moved(mine, "x", i), "a", j), "b", k))
    pl.semaphore_signal(barrier, inc=1, device_id=sib, device_id_type=MESH)
    for p in peers:
        pl.semaphore_signal(barrier, inc=1, device_id=p, device_id_type=MESH)
    pl.semaphore_wait(barrier, chips)

    sends = []
    swaps = []
    for mat, w in enumerate((gate, up)):
        s = pltpu.make_async_remote_copy(
            w.at[:, theirs], stage.at[mat, c], swap_send.at[mat], swap_recv.at[mat],
            device_id=sib, device_id_type=MESH,
        )
        s.start()
        swaps.append(s)

    def weight_slot(mat, span):
        start, width = spans[span]

        def get(chip):
            at = pl.ds(pl.multiple_of(chip * 2 * depth, 16), 2 * depth)
            return wide.at[mat, at, pl.ds(start, width)]

        return get

    items = []
    orders = ((("a", "x", "b"), ("a", "b", "x")),) * 2
    weights = []
    for span in range(len(spans)):
        weights.append((len(items), len(items) + 1))
        for mat in range(2):
            items.append((weight_slot(mat, span), orders[span][mat]))

    line = (
        a,
        a + 1 - 2 * lax.rem(a, 2),
        jnp.where(a < A // 2, 2, 1),
        jnp.where(a < A // 2, A - 1, 0),
    )
    onward = tuple(2 * a - s if n == 1 else jnp.where(s < a, a + 1, a - 1) for n, s in enumerate(line))
    all_at = [
        {"x": i, "a": j, "b": k} for i in range(X) for j in range(A) for k in range(B)
    ]

    def place_of(rel):
        return {
            "x": lax.rem(x + rel["x"], X), "a": line[rel["a"]], "b": lax.rem(b + rel["b"], B)
        }

    def hops(rel):
        return rel["x"] + rel["a"] + rel["b"]

    count = [0]

    def push(n, chip, to, when):
        ref = items[n][0](chip)
        d = pltpu.make_async_remote_copy(
            ref, ref, i_send.at[count[0]], i_recv.at[n, chip], device_id=to, device_id_type=MESH
        )
        count[0] += 1
        sends.append((d, when))
        if when is None:
            d.start()
        else:
            pl.when(when)(d.start)

    def spread(n, rel):
        order = items[n][1]
        last = max([order.index(k) for k in order if rel[k]], default=-1)
        chip = chip_of(place_of(rel))
        for axis in order[max(last, 0):]:
            if axis == "a":
                if rel["a"] == 0:
                    push(n, chip, {"a": jnp.minimum(a + 1, A - 1)}, a + 1 < A)
                    push(n, chip, {"a": jnp.maximum(a - 1, 0)}, a > 0)
                else:
                    to = onward[rel["a"]]
                    push(n, chip, {"a": jnp.clip(to, 0, A - 1)}, (to >= 0) & (to < A))
            elif rel[axis] == 0:
                push(n, chip, {axis: 1 - mine[axis]}, None)

    def arrived(n, rel):
        chip = chip_of(place_of(rel))
        ref = items[n][0](chip)
        pltpu.make_async_remote_copy(
            ref, ref, i_send.at[0], i_recv.at[n, chip], device_id=sib, device_id_type=MESH
        ).wait_recv()

    def passes(n, rel):
        return hops(rel) > 0 and rel[items[n][1][2]] == 0

    def begin(ns):
        for n in ns:
            spread(n, all_at[0])

    def stage_of(ns, h):
        for n in ns:
            for rel in all_at:
                if hops(rel) == h and passes(n, rel):
                    arrived(n, rel)
                    spread(n, rel)

    def finish(ns):
        for n in ns:
            for rel in all_at:
                if hops(rel) and not passes(n, rel):
                    arrived(n, rel)

    partners = [(j, k) for j in range(A) for k in range(B) if j or k]

    def partner(n):
        return {"a": line[partners[n][0]], "b": lax.rem(b + partners[n][1], B)}

    def mp_of(at):
        return at["a"] * B + at["b"]

    for n in range(len(partners)):
        d = pltpu.make_async_remote_copy(
            picks.at[mp_of(partner(n))], asked.at[my_mp], q_send.at[n], q_recv.at[my_mp],
            device_id=partner(n), device_id_type=MESH,
        )
        d.start()
        sends.append((d, None))

    def chosen_map(asks):
        pick = asks[:1, :1]
        got = maps[0]
        for k in range(1, maps.shape[0]):
            got = jnp.where(pick == k, maps[k], got)
        return got

    def send_adapters():
        for d in own_ads:
            d.wait()
        for n in range(len(partners)):
            who = mp_of(partner(n))
            pltpu.make_async_remote_copy(
                picks.at[who], asked.at[who], q_send.at[n], q_recv.at[who],
                device_id=sib, device_id_type=MESH,
            ).wait_recv()
        for n in reversed(range(len(partners))):
            chosen_out[n] = chosen_map(asked[mp_of(partner(n))])
            d = pltpu.make_async_remote_copy(
                chosen_out.at[n], chosen_in.at[my_mp], m_send.at[n], m_recv.at[my_mp],
                device_id=partner(n), device_id_type=MESH,
            )
            d.start()
            sends.append((d, None))
        chosen_in[my_mp] = chosen_map(picks[my_mp])

    def adapters_here():
        for n in range(len(partners)):
            who = mp_of(partner(n))
            pltpu.make_async_remote_copy(
                chosen_out.at[n], chosen_in.at[who], m_send.at[n], m_recv.at[who],
                device_id=sib, device_id_type=MESH,
            ).wait_recv()

    def join_halves():
        for mat in range(2):
            own_halves[mat].wait()
            swaps[mat].wait()
            joined = jnp.concatenate(
                [stage[mat, 0].astype(f32), stage[mat, 1].astype(f32)], axis=0
            ).astype(bf16)
            wide[mat, pl.ds(pl.multiple_of(me * 2 * depth, 16), 2 * depth), :] = joined
    def norm_rows():
        loads[0].wait()

        @pl.loop(0, tok_dev, step=PAIR)
        def _(r):
            part = pl.ds(pl.multiple_of(r, PAIR), PAIR)
            wf = tok[part, :].astype(f32)
            scale = lax.rsqrt(jnp.mean(wf * wf, axis=-1, keepdims=True) + EPSILON)
            normed[part, :] = (wf * scale * gain1[...].reshape(1, span_embed)).astype(bf16)

    def project(k, to):
        loads[(2, 1, 3)[k]].wait()

        @pl.loop(0, tok_dev, step=256)
        def _(r):
            part = pl.ds(pl.multiple_of(r, 256), 256)
            to[part, :] = jnp.dot(
                normed[part, :], wqkv[k], preferred_element_type=f32
            ).astype(to.dtype)

    column = lax.broadcasted_iota(jnp.int32, (1, heads_wide), 1)

    def pair_step(pair, carry):
        for n in range(2):
            r = pair * 2 + n
            part = pl.ds(pl.multiple_of(r * SLOTR, SLOTR), SLOTR)
            owner = slot_of[r] // maps.shape[0]
            codes = lax.dot_general(
                normed[part, :], chosen_in[owner, :, :embed],
                (((1,), (1,)), ((), ())), preferred_element_type=f32,
            ).astype(bf16)
            g = chosen_in[owner, :, embed:]
            lane = lax.broadcasted_iota(jnp.int32, codes.shape, 1)
            none = jnp.zeros_like(codes)
            for low, base, to in ((True, qf, qb), (False, vf, vb)):
                kept = jnp.where((lane < LATENT_BREADTH) == low, codes, none)
                delta = jnp.dot(kept, g, preferred_element_type=f32) * PLUGIN_STRENGTH
                to[part, :] = (base[part, :] + delta.astype(bf16).astype(f32)).astype(bf16)
        part = pl.ds(pl.multiple_of(pair * PAIR, PAIR), PAIR)
        i = lax.broadcasted_iota(jnp.int32, (PAIR, PAIR), 0)
        j = lax.broadcasted_iota(jnp.int32, (PAIR, PAIR), 1)
        len0, len1 = lens[pair * 2], lens[pair * 2 + 1]
        qi = jnp.where(i < SLOTR, i, i - SLOTR)
        kj = jnp.where(j < SLOTR, j, j - SLOTR)
        same = (i < SLOTR) == (j < SLOTR)
        live = kj < jnp.where(j < SLOTR, len0, len1)
        seen = same & live & (kj <= qi) & ((qi - kj < WINDOW) | (kj < SINKS))
        row = lax.broadcasted_iota(jnp.int32, (PAIR, 1), 0)
        alive = jnp.where(row < SLOTR, row, row - SLOTR) < jnp.where(row < SLOTR, len0, len1)
        before = None
        for h in range(HEADS):
            lo, hi = h * HD, (h + 1) * HD
            first, last = lo // LANES, (hi - 1) // LANES
            cols = slice(first * LANES, (last + 1) * LANES)
            q = qb[part, cols]
            pick = (column[:, cols] >= lo) & (column[:, cols] < hi)
            q = jnp.where(pick, q, jnp.zeros_like(q))
            s = lax.dot_general(
                q, kb[part, cols], (((1,), (1,)), ((), ())), preferred_element_type=f32
            ) * HD ** (-0.5)
            s = jnp.where(seen, s, NEVER)
            e = jnp.where(seen, jnp.exp(s - jnp.max(s, axis=-1, keepdims=True)), 0.0)
            p = (e / jnp.sum(e, axis=-1, keepdims=True)).astype(bf16)
            o = jnp.dot(p, vb[part, cols], preferred_element_type=f32)
            o = jnp.where(alive, o, 0.0).astype(bf16)
            if h > 0:
                w = h - 1
                at = column[:, w * LANES:(w + 1) * LANES]
                att[part, w * LANES:(w + 1) * LANES] = jnp.where(at < lo, before, o[:, :LANES])
            before = o[:, -LANES:]
        return carry

    def attend_pairs(first, last):
        lax.fori_loop(first, last, pair_step, 0)

    group = source.shape[1]
    ahead = lax.broadcasted_iota(jnp.int32, (group, group), 0)
    turn = jnp.where(ahead == source[...], 1.0, 0.0).astype(bf16)

    def project_out():
        loads[4].wait()

        @pl.loop(0, tok_dev, step=PAIR)
        def _(r):
            part = pl.ds(pl.multiple_of(r, PAIR), PAIR)
            mixed = tok[part, :].astype(f32) + jnp.dot(
                att[part, :], wout[...], preferred_element_type=f32
            )
            mixed = mixed.astype(bf16)
            tok[part, :] = mixed
            wf = mixed.astype(f32)
            scale = lax.rsqrt(jnp.mean(wf * wf, axis=-1, keepdims=True) + EPSILON)
            nb = (wf * scale * gain2[...].reshape(1, span_embed)).astype(bf16)
            for g in range(span_embed // group):
                cols = slice(g * group, (g + 1) * group)
                act[part, cols] = jnp.dot(nb[:, cols], turn, preferred_element_type=f32).astype(bf16)

    res = pltpu.make_async_copy(tok, res_out, res_sem.at[0])
    own_rows = pltpu.make_async_copy(shuf.at[x, :, a, b], rows.at[:, x, c, a, b], r_recv.at[me])
    block = rows.shape[5]
    def regroup():
        res.start()
        size = A * B * block
        for i in range(X):
            for k in range(CORES):
                n = i * CORES + k
                rank = lax.broadcasted_iota(jnp.int32, (tok_dev, size), 0)
                one = jnp.where(rank == want[:, n * size:(n + 1) * size], 1.0, 0.0).astype(bf16)
                ordered = lax.dot_general(
                    one, act[...], (((0,), (0,)), ((), ())), preferred_element_type=f32
                ).astype(bf16)
                shuf[i, k] = ordered.reshape(A, B, block, span_embed)

        for k, p in enumerate(peers):
            d = pltpu.make_async_remote_copy(
                shuf.at[p["x"], :, p["a"], p["b"]], rows.at[:, x, c, a, b], r_send.at[k], r_recv.at[me],
                device_id=p, device_id_type=MESH,
            )
            d.start()
            sends.append((d, None))
        own_rows.start()

    def forward_rows(p, k):
        here = rows.at[:, p["x"], c, p["a"], p["b"]]
        d = pltpu.make_async_remote_copy(
            here, here, f_send.at[k], f_recv.at[k], device_id=sib, device_id_type=MESH
        )
        d.start()
        sends.append((d, None))

    def share_rows():
        own_rows.wait()
        forward_rows(mine, chips - 1)
        for k, p in enumerate(peers):
            here = rows.at[:, p["x"], c, p["a"], p["b"]]
            pltpu.make_async_remote_copy(
                here, here, r_send.at[k], r_recv.at[chip_of(p)], device_id=sib, device_id_type=MESH
            ).wait_recv()
            forward_rows(p, k)

    def rows_shared():
        for k, p in enumerate(peers + [mine]):
            here = rows.at[:, p["x"], 1 - c, p["a"], p["b"]]
            pltpu.make_async_remote_copy(
                here, here, f_send.at[k], f_recv.at[k], device_id=sib, device_id_type=MESH
            ).wait_recv()

    def result(strip, part):
        cols = pl.ds(pl.multiple_of(c * half + strip * STRIP, STRIP), STRIP)
        at = lax.rem(strip, 2)
        if part == 0:
            return pltpu.make_async_remote_copy(
                held.at[at, 0], hid_out.at[:, cols], o_send.at[at], o_recv.at[strip],
                device_id=sib, device_id_type=MESH,
            )
        return pltpu.make_async_copy(held.at[at, 1], hid_out.at[:, cols], o_own.at[at])

    def strip_step(strip, carry):
        @pl.when(strip >= 2)
        def _():
            result(strip - 2, 0).wait_send()
            result(strip - 2, 1).wait()

        cols = pl.ds(pl.multiple_of(strip * STRIP, STRIP), STRIP)
        for part in range(2):
            who = 1 - c if part == 0 else c
            mlp_in = rows[who].reshape(tok_dev, span_embed)
            g = jnp.dot(mlp_in, wide[0, :, cols], preferred_element_type=f32)
            u = jnp.dot(mlp_in, wide[1, :, cols], preferred_element_type=f32)
            held[lax.rem(strip, 2), part] = (g * jax.nn.sigmoid(g) * u).astype(bf16)
            result(strip, part).start()
        return carry

    def hidden_units(span):
        start, width = spans[span]
        finish(weights[span])
        lax.fori_loop(start // STRIP, (start + width) // STRIP, strip_step, 0)

    norm_rows()
    send_adapters()
    join_halves()
    begin(weights[1])
    begin(weights[0])
    project(1, kb)
    stage_of(weights[1], 1)
    stage_of(weights[0], 1)
    project(0, qf)
    project(2, vf)
    stage_of(weights[1], 2)
    stage_of(weights[0], 2)
    adapters_here()
    attend_pairs(0, 2)
    stage_of(weights[1], 3)
    attend_pairs(2, 4)
    stage_of(weights[0], 3)
    project_out()
    regroup()
    stage_of(weights[0], 4)
    stage_of(weights[1], 4)
    share_rows()
    rows_shared()
    hidden_units(0)
    hidden_units(1)
    strips = half // STRIP
    for s in (strips - 2, strips - 1):
        result(jnp.int32(s), 0).wait_send()
        result(jnp.int32(s), 1).wait()
    for s in range(strips):
        result(jnp.int32(s), 0).wait_recv()
    res.wait()
    for d, when in sends:
        if when is None:
            d.wait_send()
        else:
            pl.when(when)(d.wait_send)


def layer(shape, lens, chosen, stored, tokens, wq, wk, wv, wo, shrink, grow, gate, up, gain1, gain2, want, source):
    X, A, B = shape
    chips = X * A * B
    tok_dev, depth = tokens.shape
    heads_wide = wq.shape[1]
    shard, width = gate.shape
    half = width // CORES
    block = tok_dev // (chips * CORES)
    spans = ((0, 768), (768, half - 768))
    n_items = 2 * len(spans)
    resident, rank = shrink.shape[:2]
    DMA = pltpu.SemaphoreType.DMA
    bf16 = jnp.bfloat16
    f32 = jnp.float32
    ANY = pl.BlockSpec(memory_space=pl.ANY)
    VM = pl.BlockSpec(memory_space=pltpu.VMEM)
    SM = pl.BlockSpec(memory_space=pltpu.SMEM)
    return pl.pallas_call(
        functools.partial(layer_kernel, shape, spans),
        out_shape=(
            jax.ShapeDtypeStruct((tok_dev, depth), bf16),
            jax.ShapeDtypeStruct((tok_dev, width), bf16),
        ),
        in_specs=[SM] * 3 + [ANY] * 9 + [VM] * 4,
        out_specs=(ANY, ANY),
        scratch_shapes=[
            pltpu.VMEM((tok_dev, depth), bf16),
            pltpu.VMEM((3, depth, heads_wide), bf16),
            pltpu.VMEM((heads_wide, depth), bf16),
            pltpu.VMEM((tok_dev, depth), bf16),
            pltpu.VMEM((tok_dev, heads_wide), f32),
            pltpu.VMEM((tok_dev, heads_wide), f32),
            pltpu.VMEM((tok_dev, heads_wide), bf16),
            pltpu.VMEM((tok_dev, heads_wide), bf16),
            pltpu.VMEM((tok_dev, heads_wide), bf16),
            pltpu.VMEM((tok_dev, heads_wide), bf16),
            pltpu.VMEM((tok_dev, depth), bf16),
            pltpu.VMEM((X, CORES, A, B, block, depth), bf16),
            pltpu.SMEM((chosen.shape[0],), jnp.int32),
            pltpu.VMEM((resident, rank, depth + heads_wide), bf16),
            pltpu.VMEM((A * B, 8, LANES), jnp.int32),
            pltpu.VMEM((A * B, 8, LANES), jnp.int32),
            pltpu.VMEM((A * B - 1, rank, depth + heads_wide), bf16),
            pltpu.VMEM((A * B, rank, depth + heads_wide), bf16),
            pltpu.VMEM((2, CORES, shard, half), bf16),
            pltpu.VMEM((2, depth, half), bf16),
            pltpu.VMEM((CORES, X, CORES, A, B, block, depth), bf16),
            pltpu.VMEM((2, 2, tok_dev, STRIP), bf16),
            DMA((5,)), DMA((2,)), DMA((2,)), DMA((2,)), DMA((2,)),
            DMA((n_items * 2 * chips,)), DMA((n_items, chips)),
            DMA((A * B - 1,)), DMA((A * B,)), DMA((A * B - 1,)), DMA((A * B,)),
            DMA((chips,)), DMA((chips,)), DMA((chips,)), DMA((chips,)),
            DMA((2,)), DMA((2,)), DMA((half // STRIP,)), DMA((1,)),
        ],
        compiler_params=pltpu.CompilerParams(
            collective_id=0, has_side_effects=True, vmem_limit_bytes=62 << 20
        ),
        name="layer",
    )(lens, chosen, stored, tokens, wq, wk, wv, wo, shrink, grow, gate, up, gain1, gain2, want, source)


def local_fused(
    tokens, first_norm_gain, query_weight, key_weight, value_weight, output_weight, lengths,
    request_adapter, slot_adapter_ids, plugin_shrink_maps, plugin_grow_maps, device_token_order,
    second_norm_gain, gate_weight, up_weight,
):
    shape = tuple(lax.axis_size(n) for n in ("x", "a", "b"))
    mp = shape[1] * shape[2]
    resident = plugin_shrink_maps.shape[0]
    shard = gate_weight.shape[0]
    source = np.arange(CORES * mp * shard).reshape(CORES, mp, shard).transpose(1, 0, 2)
    return layer(
        shape, lengths, request_adapter, slot_adapter_ids, tokens, query_weight, key_weight, value_weight, output_weight,
        plugin_shrink_maps.transpose(0, 2, 1),
        plugin_grow_maps.reshape(resident, 2 * LATENT_BREADTH, -1),
        gate_weight, up_weight, first_norm_gain, second_norm_gain,
        device_token_order, jnp.asarray(source.reshape(1, -1), jnp.int32),
    )


def solution(mesh):
    dp, mp = mesh.devices.shape
    fast = 1
    while fast * fast * 4 <= mp:
        fast *= 2
    devices = dp * mp
    fits = (
        EMBED_SPAN // devices * CORES % 16 == 0
        and TOK_DEV // devices % 16 == 0
        and dp == APD
        and mp == 2 * APD
    )
    if fits:
        names = ("a", "b")
        fine = jax.sharding.Mesh(
            mesh.devices.reshape(dp // CORES, CORES, mp // fast, fast), ("x", "core", "a", "b")
        )
    else:
        names = ("mp",)
        fine = jax.sharding.Mesh(
            mesh.devices.reshape(dp // CORES, CORES, mp), ("x", "core", "mp")
        )
    rows = ("x", "core") + names
    return jax.shard_map(
        local_fused if fits else local_plain,
        mesh=fine,
        in_specs=(
            P(rows, None),
            P(),
            P(),
            P(),
            P(),
            P(),
            P(rows),
            P(rows),
            P(),
            P(names, None, None),
            P(names, None, None, None),
            P(rows, None),
            P(),
            P(rows, None),
            P(rows, None),
        ),
        out_specs=(P(rows, None), P(rows, None)),
        check_vma=False,
    )
```

```python
import functools

import jax
import jax.numpy as jnp
import numpy as np
from jax import lax
from jax.experimental import pallas as pl
from jax.experimental.pallas import tpu as pltpu
from jax.sharding import PartitionSpec as P

EMBED_SPAN = 1792
HEADS = 8
HD = 112
LATENT_BREADTH = 16
REQ_DEV = 8
TOK_DEV = 512
APD = 4
SLOTR = 64
WINDOW = 32
SINKS = 4


PLUGIN_STRENGTH = 2.0
EPSILON = 1e-05


def normalize(rows_in, gain_vec):
    floated = rows_in.astype(jnp.float32)
    scale = lax.rsqrt(jnp.mean(floated * floated, axis=-1, keepdims=True) + EPSILON)
    return (floated * scale * gain_vec).astype(jnp.bfloat16)


def attend(query, key, value, request_len):
    queries = query.reshape(REQ_DEV, SLOTR, HEADS, HD)
    head_keys = key.reshape(REQ_DEV, SLOTR, HEADS, HD)
    head_values = value.reshape(REQ_DEV, SLOTR, HEADS, HD)
    scores = jnp.einsum(
        "rqhd,rkhd->rhqk", queries, head_keys, preferred_element_type=jnp.float32
    ) * HD ** (-0.5)
    places = jnp.arange(SLOTR)
    query_place = places[:, None]
    key_place = places[None, :]
    allowed = (key_place <= query_place) & (
        (query_place - key_place < WINDOW) | (key_place < SINKS)
    )
    key_live = places[None, :] < request_len[:, None]
    visible_lookup_flags = allowed[None, None, :, :] & key_live[:, None, None, :]
    scores = jnp.where(visible_lookup_flags, scores, -1e30)
    row_max = jnp.max(scores, axis=-1, keepdims=True)
    expo = jnp.where(visible_lookup_flags, jnp.exp(scores - row_max), 0.0)
    softmax_w = (expo / jnp.sum(expo, axis=-1, keepdims=True)).astype(jnp.bfloat16)
    attended = jnp.einsum(
        "rhqk,rkhd->rqhd", softmax_w, head_values, preferred_element_type=jnp.float32
    ).astype(jnp.bfloat16)
    query_live = (places[None, :] < request_len[:, None])[:, :, None, None]
    attended = jnp.where(query_live, attended, jnp.zeros_like(attended))
    return attended.reshape(REQ_DEV * SLOTR, HEADS * HD)


CORES = 2


def gate_kernel(rows_ref, gain_ref, w_ref, act_ref, o_ref):
    @pl.when(pl.program_id(0) == 0)
    def _():
        @pl.loop(0, rows_ref.shape[0], step=64)
        def _(r):
            part = pl.ds(pl.multiple_of(r, 64), 64)
            wide = rows_ref[part, :].astype(jnp.float32)
            scale = lax.rsqrt(jnp.mean(wide * wide, axis=-1, keepdims=True) + EPSILON)
            act_ref[part, :] = (wide * scale * gain_ref[...]).astype(jnp.bfloat16)

    gate = jnp.dot(act_ref[...], w_ref[...], preferred_element_type=jnp.float32)
    o_ref[...] = gate * jax.nn.sigmoid(gate)


def gate_units(regrouped, gain, weight):
    rows, depth = regrouped.shape
    width = weight.shape[1]
    tile = 512
    whole = lambda i: (0, 0)
    strip = lambda i: (0, i)
    return pl.pallas_call(
        gate_kernel,
        out_shape=(
            jax.ShapeDtypeStruct((rows, depth), jnp.bfloat16),
            jax.ShapeDtypeStruct((rows, width), jnp.float32),
        ),
        grid=(width // tile,),
        in_specs=[
            pl.BlockSpec((rows, depth), whole),
            pl.BlockSpec((1, depth), whole),
            pl.BlockSpec((depth, tile), strip),
        ],
        out_specs=(pl.BlockSpec((rows, depth), whole), pl.BlockSpec((rows, tile), strip)),
        compiler_params=pltpu.CompilerParams(vmem_limit_bytes=32 << 20),
        name="gate_units",
    )(regrouped, gain[None, :], weight)


def up_kernel(act_ref, silu_ref, w_ref, o_ref):
    up = jnp.dot(act_ref[...], w_ref[...], preferred_element_type=jnp.float32)
    o_ref[...] = (silu_ref[...] * up).astype(o_ref.dtype)


def up_units(act, silu, weight):
    rows, depth = act.shape
    width = weight.shape[1]
    tile = 512
    strip = lambda i: (0, i)
    return pl.pallas_call(
        up_kernel,
        out_shape=jax.ShapeDtypeStruct((rows, width), jnp.bfloat16),
        grid=(width // tile,),
        in_specs=[
            pl.BlockSpec((rows, depth), lambda i: (0, 0)),
            pl.BlockSpec((rows, tile), strip),
            pl.BlockSpec((depth, tile), strip),
        ],
        out_specs=pl.BlockSpec((rows, tile), strip),
        compiler_params=pltpu.CompilerParams(vmem_limit_bytes=48 << 20),
        name="up_units",
    )(act, silu, weight)


def local_plain(
    tokens,
    first_norm_gain,
    query_weight,
    key_weight,
    value_weight,
    output_weight,
    lengths,
    request_adapter,
    slot_adapter_ids,
    plugin_shrink_maps,
    plugin_grow_maps,
    device_token_order,
    second_norm_gain,
    gate_weight,
    up_weight,
):
    owner_count = lax.axis_size("mp")
    resident_slots = plugin_shrink_maps.shape[0]
    tok_dev = tokens.shape[0]
    hw_size = query_weight.shape[1]
    every = ("x", "core", "mp")

    gate_full = lax.all_gather(gate_weight, every, axis=0, tiled=True)
    up_full = lax.all_gather(up_weight, every, axis=0, tiled=True)

    matches = (slot_adapter_ids[None, :] == request_adapter[:, None]).astype(jnp.int32)
    slot_ids = jnp.sum(
        matches * jnp.arange(slot_adapter_ids.shape[0], dtype=jnp.int32)[None, :], axis=1
    )
    owner_index = slot_ids // resident_slots
    within = slot_ids % resident_slots
    routing = (jnp.arange(owner_count)[:, None] == owner_index[None, :]).astype(jnp.bfloat16)
    slot_pick = (jnp.arange(resident_slots)[None, :] == within[:, None]).astype(jnp.bfloat16)
    chosen = jnp.dot(routing, slot_pick, preferred_element_type=jnp.float32).astype(jnp.bfloat16)
    chosen_adapter = lax.all_to_all(chosen, "mp", split_axis=0, concat_axis=0, tiled=True)
    maps = jnp.concatenate(
        [
            plugin_shrink_maps.transpose(0, 2, 1),
            plugin_grow_maps.reshape(resident_slots, 2 * LATENT_BREADTH, hw_size),
        ],
        axis=-1,
    )
    outgoing = jnp.einsum(
        "ge,ezc->gzc", chosen_adapter, maps, preferred_element_type=jnp.float32
    ).astype(jnp.bfloat16)
    incoming = lax.all_to_all(outgoing, "mp", split_axis=0, concat_axis=0, tiled=True)
    own_maps = jnp.einsum(
        "or,ozc->rzc", routing, incoming, preferred_element_type=jnp.float32
    ).astype(jnp.bfloat16)

    normed = normalize(tokens, first_norm_gain)
    request_rows = normed.reshape(REQ_DEV, SLOTR, EMBED_SPAN)
    codes = jnp.einsum(
        "rsd,rkd->rsk",
        request_rows,
        own_maps[..., :EMBED_SPAN],
        preferred_element_type=jnp.float32,
    ).astype(jnp.bfloat16)
    delta_q = (
        jnp.einsum(
            "rsk,rkh->rsh",
            codes[..., :LATENT_BREADTH],
            own_maps[:, :LATENT_BREADTH, EMBED_SPAN:],
            preferred_element_type=jnp.float32,
        )
        * PLUGIN_STRENGTH
    ).astype(jnp.bfloat16)
    delta_v = (
        jnp.einsum(
            "rsk,rkh->rsh",
            codes[..., LATENT_BREADTH:],
            own_maps[:, LATENT_BREADTH:, EMBED_SPAN:],
            preferred_element_type=jnp.float32,
        )
        * PLUGIN_STRENGTH
    ).astype(jnp.bfloat16)
    query = (
        jnp.dot(normed, query_weight, preferred_element_type=jnp.float32)
        + delta_q.reshape(tok_dev, hw_size).astype(jnp.float32)
    ).astype(jnp.bfloat16)
    key = jnp.dot(normed, key_weight, preferred_element_type=jnp.float32).astype(jnp.bfloat16)
    value = (
        jnp.dot(normed, value_weight, preferred_element_type=jnp.float32)
        + delta_v.reshape(tok_dev, hw_size).astype(jnp.float32)
    ).astype(jnp.bfloat16)
    attended = attend(query, key, value, lengths)
    residual = (
        tokens.astype(jnp.float32)
        + jnp.dot(attended, output_weight, preferred_element_type=jnp.float32)
    ).astype(jnp.bfloat16)
    order = device_token_order.reshape(-1, 1) == jnp.arange(tok_dev)[None, :]
    shuffled = jnp.dot(
        order.astype(jnp.bfloat16), residual, preferred_element_type=jnp.float32
    ).astype(jnp.bfloat16)
    regrouped = lax.all_to_all(shuffled, every, split_axis=0, concat_axis=0, tiled=True)
    act, silu = gate_units(regrouped, second_norm_gain, gate_full)
    hidden = up_units(act, silu, up_full)
    return (residual, hidden)


MESH = pl.DeviceIdType.MESH
STRIP = 256
PAIR = 2 * SLOTR
LANES = 128
NEVER = -1e30


def layer_kernel(
    shape, spans,
    lens, chosen, stored, tokens, wq, wk, wv, wo, shrink, grow, gate, up, gain1, gain2, want, source,
    res_out, hid_out,
    tok, wqkv, wout, normed, qf, vf, kb, qb, vb, att, act, shuf,
    slot_of, maps, picks, asked, chosen_out, chosen_in, stage, wide, rows, held,
    load_sem, ad_sem, swap_send, swap_recv, swap_own, i_send, i_recv, q_send, q_recv, m_send, m_recv,
    r_send, r_recv, f_send, f_recv, o_own, o_send, o_recv, res_sem,
):
    X, A, B = shape
    x, c, a, b = (lax.axis_index(n) for n in ("x", "core", "a", "b"))
    sib = {"core": 1 - c}
    sizes = {"x": X, "a": A, "b": B}
    mine = {"x": x, "a": a, "b": b}
    depth = gate.shape[0]
    half = wide.shape[2]
    chips = X * A * B
    tok_dev = tok.shape[0]
    span_embed = tok.shape[1]
    heads_wide = kb.shape[1]
    f32 = jnp.float32
    bf16 = jnp.bfloat16

    def chip_of(at):
        return (at["x"] * A + at["a"]) * B + at["b"]

    def moved(at, axis, k):
        return {**at, axis: lax.rem(at[axis] + k, sizes[axis])}

    me = chip_of(mine)
    group_size = A * B
    my_mp = a * B + b
    embed = shrink.shape[2]
    loads = []
    own_ads = []
    for k, (frm, to) in enumerate(
        ((shrink, maps.at[:, :, :embed]), (grow, maps.at[:, :, embed:]))
    ):
        d = pltpu.make_async_copy(frm, to, ad_sem.at[k])
        d.start()
        own_ads.append(d)
    for k, (frm, to) in enumerate(
        ((tokens, tok), (wk, wqkv.at[1]), (wq, wqkv.at[0]), (wv, wqkv.at[2]), (wo, wout))
    ):
        d = pltpu.make_async_copy(frm, to, load_sem.at[k])
        d.start()
        loads.append(d)
    theirs = pl.ds(pl.multiple_of((1 - c) * half, half), half)
    ours = pl.ds(pl.multiple_of(c * half, half), half)
    own_halves = []
    for mat, w in enumerate((gate, up)):
        d = pltpu.make_async_copy(w.at[:, ours], stage.at[mat, c], swap_own.at[mat])
        d.start()
        own_halves.append(d)

    count_req = chosen.shape[0]

    def look(s, got):
        here = stored[s]
        return tuple(jnp.where(here == chosen[r], s, g) for r, g in enumerate(got))

    found = lax.fori_loop(0, stored.shape[0], look, (jnp.int32(0),) * count_req)
    for r, s in enumerate(found):
        slot_of[r] = s
    for m in range(group_size):
        ask = jnp.int32(0)
        for s in found:
            ask = jnp.where(s // maps.shape[0] == m, s % maps.shape[0], ask)
        picks[m] = jnp.full(picks.shape[1:], ask, jnp.int32)

    barrier = pltpu.get_barrier_semaphore()
    peers = []
    for i in range(X):
        for j in range(A):
            for k in range(B):
                if i or j or k:
                    peers.append(moved(moved(moved(mine, "x", i), "a", j), "b", k))
    pl.semaphore_signal(barrier, inc=1, device_id=sib, device_id_type=MESH)
    for p in peers:
        pl.semaphore_signal(barrier, inc=1, device_id=p, device_id_type=MESH)
    pl.semaphore_wait(barrier, chips)

    sends = []
    swaps = []
    for mat, w in enumerate((gate, up)):
        s = pltpu.make_async_remote_copy(
            w.at[:, theirs], stage.at[mat, c], swap_send.at[mat], swap_recv.at[mat],
            device_id=sib, device_id_type=MESH,
        )
        s.start()
        swaps.append(s)

    def weight_slot(mat, span):
        start, width = spans[span]

        def get(chip):
            at = pl.ds(pl.multiple_of(chip * 2 * depth, 16), 2 * depth)
            return wide.at[mat, at, pl.ds(start, width)]

        return get

    items = []
    orders = ((("a", "x", "b"), ("a", "b", "x")), (("a", "x", "b"), ("b", "a", "x")),)
    weights = []
    for span in range(len(spans)):
        weights.append((len(items), len(items) + 1))
        for mat in range(2):
            items.append((weight_slot(mat, span), orders[span][mat]))

    line = (
        a,
        a + 1 - 2 * lax.rem(a, 2),
        jnp.where(a < A // 2, 2, 1),
        jnp.where(a < A // 2, A - 1, 0),
    )
    onward = tuple(2 * a - s if n == 1 else jnp.where(s < a, a + 1, a - 1) for n, s in enumerate(line))
    all_at = [
        {"x": i, "a": j, "b": k} for i in range(X) for j in range(A) for k in range(B)
    ]

    def place_of(rel):
        return {
            "x": lax.rem(x + rel["x"], X), "a": line[rel["a"]], "b": lax.rem(b + rel["b"], B)
        }

    def hops(rel):
        return rel["x"] + rel["a"] + rel["b"]

    count = [0]

    def push(n, chip, to, when):
        ref = items[n][0](chip)
        d = pltpu.make_async_remote_copy(
            ref, ref, i_send.at[count[0]], i_recv.at[n, chip], device_id=to, device_id_type=MESH
        )
        count[0] += 1
        sends.append((d, when))
        if when is None:
            d.start()
        else:
            pl.when(when)(d.start)

    def spread(n, rel):
        order = items[n][1]
        last = max([order.index(k) for k in order if rel[k]], default=-1)
        chip = chip_of(place_of(rel))
        for axis in order[max(last, 0):]:
            if axis == "a":
                if rel["a"] == 0:
                    push(n, chip, {"a": jnp.minimum(a + 1, A - 1)}, a + 1 < A)
                    push(n, chip, {"a": jnp.maximum(a - 1, 0)}, a > 0)
                else:
                    to = onward[rel["a"]]
                    push(n, chip, {"a": jnp.clip(to, 0, A - 1)}, (to >= 0) & (to < A))
            elif rel[axis] == 0:
                push(n, chip, {axis: 1 - mine[axis]}, None)

    def arrived(n, rel):
        chip = chip_of(place_of(rel))
        ref = items[n][0](chip)
        pltpu.make_async_remote_copy(
            ref, ref, i_send.at[0], i_recv.at[n, chip], device_id=sib, device_id_type=MESH
        ).wait_recv()

    def passes(n, rel):
        return hops(rel) > 0 and rel[items[n][1][2]] == 0

    def begin(ns):
        for n in ns:
            spread(n, all_at[0])

    def stage_of(ns, h):
        for n in ns:
            for rel in all_at:
                if hops(rel) == h and passes(n, rel):
                    arrived(n, rel)
                    spread(n, rel)

    def finish(ns):
        for n in ns:
            for rel in all_at:
                if hops(rel) and not passes(n, rel):
                    arrived(n, rel)

    partners = [(j, k) for j in range(A) for k in range(B) if j or k]

    def partner(n):
        return {"a": line[partners[n][0]], "b": lax.rem(b + partners[n][1], B)}

    def mp_of(at):
        return at["a"] * B + at["b"]

    for n in range(len(partners)):
        d = pltpu.make_async_remote_copy(
            picks.at[mp_of(partner(n))], asked.at[my_mp], q_send.at[n], q_recv.at[my_mp],
            device_id=partner(n), device_id_type=MESH,
        )
        d.start()
        sends.append((d, None))

    def chosen_map(asks):
        pick = asks[:1, :1]
        got = maps[0]
        for k in range(1, maps.shape[0]):
            got = jnp.where(pick == k, maps[k], got)
        return got

    def send_adapters():
        for d in own_ads:
            d.wait()
        for n in range(len(partners)):
            who = mp_of(partner(n))
            pltpu.make_async_remote_copy(
                picks.at[who], asked.at[who], q_send.at[n], q_recv.at[who],
                device_id=sib, device_id_type=MESH,
            ).wait_recv()
        for n in reversed(range(len(partners))):
            chosen_out[n] = chosen_map(asked[mp_of(partner(n))])
            d = pltpu.make_async_remote_copy(
                chosen_out.at[n], chosen_in.at[my_mp], m_send.at[n], m_recv.at[my_mp],
                device_id=partner(n), device_id_type=MESH,
            )
            d.start()
            sends.append((d, None))
        chosen_in[my_mp] = chosen_map(picks[my_mp])

    def adapters_here():
        for n in range(len(partners)):
            who = mp_of(partner(n))
            pltpu.make_async_remote_copy(
                chosen_out.at[n], chosen_in.at[who], m_send.at[n], m_recv.at[who],
                device_id=sib, device_id_type=MESH,
            ).wait_recv()

    def join_halves():
        for mat in range(2):
            own_halves[mat].wait()
            swaps[mat].wait()
            joined = jnp.concatenate(
                [stage[mat, 0].astype(f32), stage[mat, 1].astype(f32)], axis=0
            ).astype(bf16)
            wide[mat, pl.ds(pl.multiple_of(me * 2 * depth, 16), 2 * depth), :] = joined
    def norm_rows():
        loads[0].wait()

        @pl.loop(0, tok_dev, step=PAIR)
        def _(r):
            part = pl.ds(pl.multiple_of(r, PAIR), PAIR)
            wf = tok[part, :].astype(f32)
            scale = lax.rsqrt(jnp.mean(wf * wf, axis=-1, keepdims=True) + EPSILON)
            normed[part, :] = (wf * scale * gain1[...].reshape(1, span_embed)).astype(bf16)

    def project(k, to):
        loads[(2, 1, 3)[k]].wait()

        @pl.loop(0, tok_dev, step=256)
        def _(r):
            part = pl.ds(pl.multiple_of(r, 256), 256)
            to[part, :] = jnp.dot(
                normed[part, :], wqkv[k], preferred_element_type=f32
            ).astype(to.dtype)

    column = lax.broadcasted_iota(jnp.int32, (1, heads_wide), 1)

    def pair_step(pair, carry):
        for n in range(2):
            r = pair * 2 + n
            part = pl.ds(pl.multiple_of(r * SLOTR, SLOTR), SLOTR)
            owner = slot_of[r] // maps.shape[0]
            codes = lax.dot_general(
                normed[part, :], chosen_in[owner, :, :embed],
                (((1,), (1,)), ((), ())), preferred_element_type=f32,
            ).astype(bf16)
            g = chosen_in[owner, :, embed:]
            lane = lax.broadcasted_iota(jnp.int32, codes.shape, 1)
            none = jnp.zeros_like(codes)
            for low, base, to in ((True, qf, qb), (False, vf, vb)):
                kept = jnp.where((lane < LATENT_BREADTH) == low, codes, none)
                delta = jnp.dot(kept, g, preferred_element_type=f32) * PLUGIN_STRENGTH
                to[part, :] = (base[part, :] + delta.astype(bf16).astype(f32)).astype(bf16)
        part = pl.ds(pl.multiple_of(pair * PAIR, PAIR), PAIR)
        i = lax.broadcasted_iota(jnp.int32, (PAIR, PAIR), 0)
        j = lax.broadcasted_iota(jnp.int32, (PAIR, PAIR), 1)
        len0, len1 = lens[pair * 2], lens[pair * 2 + 1]
        qi = jnp.where(i < SLOTR, i, i - SLOTR)
        kj = jnp.where(j < SLOTR, j, j - SLOTR)
        same = (i < SLOTR) == (j < SLOTR)
        live = kj < jnp.where(j < SLOTR, len0, len1)
        seen = same & live & (kj <= qi) & ((qi - kj < WINDOW) | (kj < SINKS))
        row = lax.broadcasted_iota(jnp.int32, (PAIR, 1), 0)
        alive = jnp.where(row < SLOTR, row, row - SLOTR) < jnp.where(row < SLOTR, len0, len1)
        before = None
        for h in range(HEADS):
            lo, hi = h * HD, (h + 1) * HD
            first, last = lo // LANES, (hi - 1) // LANES
            cols = slice(first * LANES, (last + 1) * LANES)
            q = qb[part, cols]
            pick = (column[:, cols] >= lo) & (column[:, cols] < hi)
            q = jnp.where(pick, q, jnp.zeros_like(q))
            s = lax.dot_general(
                q, kb[part, cols], (((1,), (1,)), ((), ())), preferred_element_type=f32
            ) * HD ** (-0.5)
            s = jnp.where(seen, s, NEVER)
            e = jnp.where(seen, jnp.exp(s - jnp.max(s, axis=-1, keepdims=True)), 0.0)
            p = (e / jnp.sum(e, axis=-1, keepdims=True)).astype(bf16)
            o = jnp.dot(p, vb[part, cols], preferred_element_type=f32)
            o = jnp.where(alive, o, 0.0).astype(bf16)
            if h > 0:
                w = h - 1
                at = column[:, w * LANES:(w + 1) * LANES]
                att[part, w * LANES:(w + 1) * LANES] = jnp.where(at < lo, before, o[:, :LANES])
            before = o[:, -LANES:]
        return carry

    def attend_pairs(first, last):
        lax.fori_loop(first, last, pair_step, 0)

    group = source.shape[1]
    ahead = lax.broadcasted_iota(jnp.int32, (group, group), 0)
    turn = jnp.where(ahead == source[...], 1.0, 0.0).astype(bf16)

    def project_out():
        loads[4].wait()

        @pl.loop(0, tok_dev, step=PAIR)
        def _(r):
            part = pl.ds(pl.multiple_of(r, PAIR), PAIR)
            mixed = tok[part, :].astype(f32) + jnp.dot(
                att[part, :], wout[...], preferred_element_type=f32
            )
            mixed = mixed.astype(bf16)
            tok[part, :] = mixed
            wf = mixed.astype(f32)
            scale = lax.rsqrt(jnp.mean(wf * wf, axis=-1, keepdims=True) + EPSILON)
            nb = (wf * scale * gain2[...].reshape(1, span_embed)).astype(bf16)
            for g in range(span_embed // group):
                cols = slice(g * group, (g + 1) * group)
                act[part, cols] = jnp.dot(nb[:, cols], turn, preferred_element_type=f32).astype(bf16)

    res = pltpu.make_async_copy(tok, res_out, res_sem.at[0])
    own_rows = pltpu.make_async_copy(shuf.at[x, :, a, b], rows.at[:, x, c, a, b], r_recv.at[me])
    block = rows.shape[5]
    def regroup():
        res.start()
        size = A * B * block
        for i in range(X):
            for k in range(CORES):
                n = i * CORES + k
                rank = lax.broadcasted_iota(jnp.int32, (tok_dev, size), 0)
                one = jnp.where(rank == want[:, n * size:(n + 1) * size], 1.0, 0.0).astype(bf16)
                ordered = lax.dot_general(
                    one, act[...], (((0,), (0,)), ((), ())), preferred_element_type=f32
                ).astype(bf16)
                shuf[i, k] = ordered.reshape(A, B, block, span_embed)

        for k, p in enumerate(peers):
            d = pltpu.make_async_remote_copy(
                shuf.at[p["x"], :, p["a"], p["b"]], rows.at[:, x, c, a, b], r_send.at[k], r_recv.at[me],
                device_id=p, device_id_type=MESH,
            )
            d.start()
            sends.append((d, None))
        own_rows.start()

    def forward_rows(p, k):
        here = rows.at[:, p["x"], c, p["a"], p["b"]]
        d = pltpu.make_async_remote_copy(
            here, here, f_send.at[k], f_recv.at[k], device_id=sib, device_id_type=MESH
        )
        d.start()
        sends.append((d, None))

    def share_rows():
        own_rows.wait()
        forward_rows(mine, chips - 1)
        for k, p in enumerate(peers):
            here = rows.at[:, p["x"], c, p["a"], p["b"]]
            pltpu.make_async_remote_copy(
                here, here, r_send.at[k], r_recv.at[chip_of(p)], device_id=sib, device_id_type=MESH
            ).wait_recv()
            forward_rows(p, k)

    def rows_shared():
        for k, p in enumerate(peers + [mine]):
            here = rows.at[:, p["x"], 1 - c, p["a"], p["b"]]
            pltpu.make_async_remote_copy(
                here, here, f_send.at[k], f_recv.at[k], device_id=sib, device_id_type=MESH
            ).wait_recv()

    def result(strip, part):
        cols = pl.ds(pl.multiple_of(c * half + strip * STRIP, STRIP), STRIP)
        at = lax.rem(strip, 2)
        if part == 0:
            return pltpu.make_async_remote_copy(
                held.at[at, 0], hid_out.at[:, cols], o_send.at[at], o_recv.at[strip],
                device_id=sib, device_id_type=MESH,
            )
        return pltpu.make_async_copy(held.at[at, 1], hid_out.at[:, cols], o_own.at[at])

    def strip_step(strip, carry):
        @pl.when(strip >= 2)
        def _():
            result(strip - 2, 0).wait_send()
            result(strip - 2, 1).wait()

        cols = pl.ds(pl.multiple_of(strip * STRIP, STRIP), STRIP)
        for part in range(2):
            who = 1 - c if part == 0 else c
            mlp_in = rows[who].reshape(tok_dev, span_embed)
            g = jnp.dot(mlp_in, wide[0, :, cols], preferred_element_type=f32)
            u = jnp.dot(mlp_in, wide[1, :, cols], preferred_element_type=f32)
            held[lax.rem(strip, 2), part] = (g * jax.nn.sigmoid(g) * u).astype(bf16)
            result(strip, part).start()
        return carry

    def hidden_units(span):
        start, width = spans[span]
        finish(weights[span])
        lax.fori_loop(start // STRIP, (start + width) // STRIP, strip_step, 0)

    join_halves()
    begin(weights[1])
    begin(weights[0])
    send_adapters()
    norm_rows()
    stage_of(weights[1], 1)
    stage_of(weights[0], 1)
    project(1, kb)
    project(0, qf)
    stage_of(weights[1], 2)
    stage_of(weights[0], 2)
    project(2, vf)
    adapters_here()
    attend_pairs(0, 1)
    stage_of(weights[1], 3)
    attend_pairs(1, 3)
    stage_of(weights[0], 3)
    attend_pairs(3, 4)
    project_out()
    regroup()
    stage_of(weights[0], 4)
    stage_of(weights[1], 4)
    share_rows()
    rows_shared()
    hidden_units(0)
    hidden_units(1)
    strips = half // STRIP
    for s in (strips - 2, strips - 1):
        result(jnp.int32(s), 0).wait_send()
        result(jnp.int32(s), 1).wait()
    for s in range(strips):
        result(jnp.int32(s), 0).wait_recv()
    res.wait()
    for d, when in sends:
        if when is None:
            d.wait_send()
        else:
            pl.when(when)(d.wait_send)


def layer(shape, lens, chosen, stored, tokens, wq, wk, wv, wo, shrink, grow, gate, up, gain1, gain2, want, source):
    X, A, B = shape
    chips = X * A * B
    tok_dev, depth = tokens.shape
    heads_wide = wq.shape[1]
    shard, width = gate.shape
    half = width // CORES
    block = tok_dev // (chips * CORES)
    spans = ((0, 768), (768, half - 768))
    n_items = 2 * len(spans)
    resident, rank = shrink.shape[:2]
    DMA = pltpu.SemaphoreType.DMA
    bf16 = jnp.bfloat16
    f32 = jnp.float32
    ANY = pl.BlockSpec(memory_space=pl.ANY)
    VM = pl.BlockSpec(memory_space=pltpu.VMEM)
    SM = pl.BlockSpec(memory_space=pltpu.SMEM)
    return pl.pallas_call(
        functools.partial(layer_kernel, shape, spans),
        out_shape=(
            jax.ShapeDtypeStruct((tok_dev, depth), bf16),
            jax.ShapeDtypeStruct((tok_dev, width), bf16),
        ),
        in_specs=[SM] * 3 + [ANY] * 9 + [VM] * 4,
        out_specs=(ANY, ANY),
        scratch_shapes=[
            pltpu.VMEM((tok_dev, depth), bf16),
            pltpu.VMEM((3, depth, heads_wide), bf16),
            pltpu.VMEM((heads_wide, depth), bf16),
            pltpu.VMEM((tok_dev, depth), bf16),
            pltpu.VMEM((tok_dev, heads_wide), f32),
            pltpu.VMEM((tok_dev, heads_wide), f32),
            pltpu.VMEM((tok_dev, heads_wide), bf16),
            pltpu.VMEM((tok_dev, heads_wide), bf16),
            pltpu.VMEM((tok_dev, heads_wide), bf16),
            pltpu.VMEM((tok_dev, heads_wide), bf16),
            pltpu.VMEM((tok_dev, depth), bf16),
            pltpu.VMEM((X, CORES, A, B, block, depth), bf16),
            pltpu.SMEM((chosen.shape[0],), jnp.int32),
            pltpu.VMEM((resident, rank, depth + heads_wide), bf16),
            pltpu.VMEM((A * B, 8, LANES), jnp.int32),
            pltpu.VMEM((A * B, 8, LANES), jnp.int32),
            pltpu.VMEM((A * B - 1, rank, depth + heads_wide), bf16),
            pltpu.VMEM((A * B, rank, depth + heads_wide), bf16),
            pltpu.VMEM((2, CORES, shard, half), bf16),
            pltpu.VMEM((2, depth, half), bf16),
            pltpu.VMEM((CORES, X, CORES, A, B, block, depth), bf16),
            pltpu.VMEM((2, 2, tok_dev, STRIP), bf16),
            DMA((5,)), DMA((2,)), DMA((2,)), DMA((2,)), DMA((2,)),
            DMA((n_items * 2 * chips,)), DMA((n_items, chips)),
            DMA((A * B - 1,)), DMA((A * B,)), DMA((A * B - 1,)), DMA((A * B,)),
            DMA((chips,)), DMA((chips,)), DMA((chips,)), DMA((chips,)),
            DMA((2,)), DMA((2,)), DMA((half // STRIP,)), DMA((1,)),
        ],
        compiler_params=pltpu.CompilerParams(
            collective_id=0, has_side_effects=True, vmem_limit_bytes=62 << 20
        ),
        name="layer",
    )(lens, chosen, stored, tokens, wq, wk, wv, wo, shrink, grow, gate, up, gain1, gain2, want, source)


def local_fused(
    tokens, first_norm_gain, query_weight, key_weight, value_weight, output_weight, lengths,
    request_adapter, slot_adapter_ids, plugin_shrink_maps, plugin_grow_maps, device_token_order,
    second_norm_gain, gate_weight, up_weight,
):
    shape = tuple(lax.axis_size(n) for n in ("x", "a", "b"))
    mp = shape[1] * shape[2]
    resident = plugin_shrink_maps.shape[0]
    shard = gate_weight.shape[0]
    source = np.arange(CORES * mp * shard).reshape(CORES, mp, shard).transpose(1, 0, 2)
    return layer(
        shape, lengths, request_adapter, slot_adapter_ids, tokens, query_weight, key_weight, value_weight, output_weight,
        plugin_shrink_maps.transpose(0, 2, 1),
        plugin_grow_maps.reshape(resident, 2 * LATENT_BREADTH, -1),
        gate_weight, up_weight, first_norm_gain, second_norm_gain,
        device_token_order, jnp.asarray(source.reshape(1, -1), jnp.int32),
    )


def solution(mesh):
    dp, mp = mesh.devices.shape
    fast = 1
    while fast * fast * 4 <= mp:
        fast *= 2
    devices = dp * mp
    fits = (
        EMBED_SPAN // devices * CORES % 16 == 0
        and TOK_DEV // devices % 16 == 0
        and dp == APD
        and mp == 2 * APD
    )
    if fits:
        names = ("a", "b")
        fine = jax.sharding.Mesh(
            mesh.devices.reshape(dp // CORES, CORES, mp // fast, fast), ("x", "core", "a", "b")
        )
    else:
        names = ("mp",)
        fine = jax.sharding.Mesh(
            mesh.devices.reshape(dp // CORES, CORES, mp), ("x", "core", "mp")
        )
    rows = ("x", "core") + names
    return jax.shard_map(
        local_fused if fits else local_plain,
        mesh=fine,
        in_specs=(
            P(rows, None),
            P(),
            P(),
            P(),
            P(),
            P(),
            P(rows),
            P(rows),
            P(),
            P(names, None, None),
            P(names, None, None, None),
            P(rows, None),
            P(),
            P(rows, None),
            P(rows, None),
        ),
        out_specs=(P(rows, None), P(rows, None)),
        check_vma=False,
    )
```

```python
import functools

import jax
import jax.numpy as jnp
import numpy as np
from jax import lax
from jax.experimental import pallas as pl
from jax.experimental.pallas import tpu as pltpu
from jax.sharding import PartitionSpec as P

EMBED_SPAN = 1792
HEADS = 8
HD = 112
LATENT_BREADTH = 16
REQ_DEV = 8
TOK_DEV = 512
APD = 4
SLOTR = 64
WINDOW = 32
SINKS = 4


PLUGIN_STRENGTH = 2.0
EPSILON = 1e-05


def normalize(rows_in, gain_vec):
    floated = rows_in.astype(jnp.float32)
    scale = lax.rsqrt(jnp.mean(floated * floated, axis=-1, keepdims=True) + EPSILON)
    return (floated * scale * gain_vec).astype(jnp.bfloat16)


def attend(query, key, value, request_len):
    queries = query.reshape(REQ_DEV, SLOTR, HEADS, HD)
    head_keys = key.reshape(REQ_DEV, SLOTR, HEADS, HD)
    head_values = value.reshape(REQ_DEV, SLOTR, HEADS, HD)
    scores = jnp.einsum(
        "rqhd,rkhd->rhqk", queries, head_keys, preferred_element_type=jnp.float32
    ) * HD ** (-0.5)
    places = jnp.arange(SLOTR)
    query_place = places[:, None]
    key_place = places[None, :]
    allowed = (key_place <= query_place) & (
        (query_place - key_place < WINDOW) | (key_place < SINKS)
    )
    key_live = places[None, :] < request_len[:, None]
    visible_lookup_flags = allowed[None, None, :, :] & key_live[:, None, None, :]
    scores = jnp.where(visible_lookup_flags, scores, -1e30)
    row_max = jnp.max(scores, axis=-1, keepdims=True)
    expo = jnp.where(visible_lookup_flags, jnp.exp(scores - row_max), 0.0)
    softmax_w = (expo / jnp.sum(expo, axis=-1, keepdims=True)).astype(jnp.bfloat16)
    attended = jnp.einsum(
        "rhqk,rkhd->rqhd", softmax_w, head_values, preferred_element_type=jnp.float32
    ).astype(jnp.bfloat16)
    query_live = (places[None, :] < request_len[:, None])[:, :, None, None]
    attended = jnp.where(query_live, attended, jnp.zeros_like(attended))
    return attended.reshape(REQ_DEV * SLOTR, HEADS * HD)


CORES = 2


def gate_kernel(rows_ref, gain_ref, w_ref, act_ref, o_ref):
    @pl.when(pl.program_id(0) == 0)
    def _():
        @pl.loop(0, rows_ref.shape[0], step=64)
        def _(r):
            part = pl.ds(pl.multiple_of(r, 64), 64)
            wide = rows_ref[part, :].astype(jnp.float32)
            scale = lax.rsqrt(jnp.mean(wide * wide, axis=-1, keepdims=True) + EPSILON)
            act_ref[part, :] = (wide * scale * gain_ref[...]).astype(jnp.bfloat16)

    gate = jnp.dot(act_ref[...], w_ref[...], preferred_element_type=jnp.float32)
    o_ref[...] = gate * jax.nn.sigmoid(gate)


def gate_units(regrouped, gain, weight):
    rows, depth = regrouped.shape
    width = weight.shape[1]
    tile = 512
    whole = lambda i: (0, 0)
    strip = lambda i: (0, i)
    return pl.pallas_call(
        gate_kernel,
        out_shape=(
            jax.ShapeDtypeStruct((rows, depth), jnp.bfloat16),
            jax.ShapeDtypeStruct((rows, width), jnp.float32),
        ),
        grid=(width // tile,),
        in_specs=[
            pl.BlockSpec((rows, depth), whole),
            pl.BlockSpec((1, depth), whole),
            pl.BlockSpec((depth, tile), strip),
        ],
        out_specs=(pl.BlockSpec((rows, depth), whole), pl.BlockSpec((rows, tile), strip)),
        compiler_params=pltpu.CompilerParams(vmem_limit_bytes=32 << 20),
        name="gate_units",
    )(regrouped, gain[None, :], weight)


def up_kernel(act_ref, silu_ref, w_ref, o_ref):
    up = jnp.dot(act_ref[...], w_ref[...], preferred_element_type=jnp.float32)
    o_ref[...] = (silu_ref[...] * up).astype(o_ref.dtype)


def up_units(act, silu, weight):
    rows, depth = act.shape
    width = weight.shape[1]
    tile = 512
    strip = lambda i: (0, i)
    return pl.pallas_call(
        up_kernel,
        out_shape=jax.ShapeDtypeStruct((rows, width), jnp.bfloat16),
        grid=(width // tile,),
        in_specs=[
            pl.BlockSpec((rows, depth), lambda i: (0, 0)),
            pl.BlockSpec((rows, tile), strip),
            pl.BlockSpec((depth, tile), strip),
        ],
        out_specs=pl.BlockSpec((rows, tile), strip),
        compiler_params=pltpu.CompilerParams(vmem_limit_bytes=48 << 20),
        name="up_units",
    )(act, silu, weight)


def local_plain(
    tokens,
    first_norm_gain,
    query_weight,
    key_weight,
    value_weight,
    output_weight,
    lengths,
    request_adapter,
    slot_adapter_ids,
    plugin_shrink_maps,
    plugin_grow_maps,
    device_token_order,
    second_norm_gain,
    gate_weight,
    up_weight,
):
    owner_count = lax.axis_size("mp")
    resident_slots = plugin_shrink_maps.shape[0]
    tok_dev = tokens.shape[0]
    hw_size = query_weight.shape[1]
    every = ("x", "core", "mp")

    gate_full = lax.all_gather(gate_weight, every, axis=0, tiled=True)
    up_full = lax.all_gather(up_weight, every, axis=0, tiled=True)

    matches = (slot_adapter_ids[None, :] == request_adapter[:, None]).astype(jnp.int32)
    slot_ids = jnp.sum(
        matches * jnp.arange(slot_adapter_ids.shape[0], dtype=jnp.int32)[None, :], axis=1
    )
    owner_index = slot_ids // resident_slots
    within = slot_ids % resident_slots
    routing = (jnp.arange(owner_count)[:, None] == owner_index[None, :]).astype(jnp.bfloat16)
    slot_pick = (jnp.arange(resident_slots)[None, :] == within[:, None]).astype(jnp.bfloat16)
    chosen = jnp.dot(routing, slot_pick, preferred_element_type=jnp.float32).astype(jnp.bfloat16)
    chosen_adapter = lax.all_to_all(chosen, "mp", split_axis=0, concat_axis=0, tiled=True)
    maps = jnp.concatenate(
        [
            plugin_shrink_maps.transpose(0, 2, 1),
            plugin_grow_maps.reshape(resident_slots, 2 * LATENT_BREADTH, hw_size),
        ],
        axis=-1,
    )
    outgoing = jnp.einsum(
        "ge,ezc->gzc", chosen_adapter, maps, preferred_element_type=jnp.float32
    ).astype(jnp.bfloat16)
    incoming = lax.all_to_all(outgoing, "mp", split_axis=0, concat_axis=0, tiled=True)
    own_maps = jnp.einsum(
        "or,ozc->rzc", routing, incoming, preferred_element_type=jnp.float32
    ).astype(jnp.bfloat16)

    normed = normalize(tokens, first_norm_gain)
    request_rows = normed.reshape(REQ_DEV, SLOTR, EMBED_SPAN)
    codes = jnp.einsum(
        "rsd,rkd->rsk",
        request_rows,
        own_maps[..., :EMBED_SPAN],
        preferred_element_type=jnp.float32,
    ).astype(jnp.bfloat16)
    delta_q = (
        jnp.einsum(
            "rsk,rkh->rsh",
            codes[..., :LATENT_BREADTH],
            own_maps[:, :LATENT_BREADTH, EMBED_SPAN:],
            preferred_element_type=jnp.float32,
        )
        * PLUGIN_STRENGTH
    ).astype(jnp.bfloat16)
    delta_v = (
        jnp.einsum(
            "rsk,rkh->rsh",
            codes[..., LATENT_BREADTH:],
            own_maps[:, LATENT_BREADTH:, EMBED_SPAN:],
            preferred_element_type=jnp.float32,
        )
        * PLUGIN_STRENGTH
    ).astype(jnp.bfloat16)
    query = (
        jnp.dot(normed, query_weight, preferred_element_type=jnp.float32)
        + delta_q.reshape(tok_dev, hw_size).astype(jnp.float32)
    ).astype(jnp.bfloat16)
    key = jnp.dot(normed, key_weight, preferred_element_type=jnp.float32).astype(jnp.bfloat16)
    value = (
        jnp.dot(normed, value_weight, preferred_element_type=jnp.float32)
        + delta_v.reshape(tok_dev, hw_size).astype(jnp.float32)
    ).astype(jnp.bfloat16)
    attended = attend(query, key, value, lengths)
    residual = (
        tokens.astype(jnp.float32)
        + jnp.dot(attended, output_weight, preferred_element_type=jnp.float32)
    ).astype(jnp.bfloat16)
    order = device_token_order.reshape(-1, 1) == jnp.arange(tok_dev)[None, :]
    shuffled = jnp.dot(
        order.astype(jnp.bfloat16), residual, preferred_element_type=jnp.float32
    ).astype(jnp.bfloat16)
    regrouped = lax.all_to_all(shuffled, every, split_axis=0, concat_axis=0, tiled=True)
    act, silu = gate_units(regrouped, second_norm_gain, gate_full)
    hidden = up_units(act, silu, up_full)
    return (residual, hidden)


MESH = pl.DeviceIdType.MESH
STRIP = 256
PAIR = 2 * SLOTR
LANES = 128
NEVER = -1e30


def layer_kernel(
    shape, spans,
    lens, chosen, stored, tokens, wq, wk, wv, wo, shrink, grow, gate, up, gain1, gain2, want, source,
    res_out, hid_out,
    tok, wqkv, wout, normed, qf, vf, kb, qb, vb, att, act, shuf,
    slot_of, maps, picks, asked, chosen_out, chosen_in, stage, wide, rows, held,
    load_sem, ad_sem, swap_send, swap_recv, swap_own, i_send, i_recv, q_send, q_recv, m_send, m_recv,
    r_send, r_recv, f_send, f_recv, o_own, o_send, o_recv, res_sem,
):
    X, A, B = shape
    x, c, a, b = (lax.axis_index(n) for n in ("x", "core", "a", "b"))
    sib = {"core": 1 - c}
    sizes = {"x": X, "a": A, "b": B}
    mine = {"x": x, "a": a, "b": b}
    depth = gate.shape[0]
    half = wide.shape[2]
    chips = X * A * B
    tok_dev = tok.shape[0]
    span_embed = tok.shape[1]
    heads_wide = kb.shape[1]
    f32 = jnp.float32
    bf16 = jnp.bfloat16

    def chip_of(at):
        return (at["x"] * A + at["a"]) * B + at["b"]

    def moved(at, axis, k):
        return {**at, axis: lax.rem(at[axis] + k, sizes[axis])}

    me = chip_of(mine)
    group_size = A * B
    my_mp = a * B + b
    embed = shrink.shape[2]
    loads = []
    own_ads = []
    for k, (frm, to) in enumerate(
        ((shrink, maps.at[:, :, :embed]), (grow, maps.at[:, :, embed:]))
    ):
        d = pltpu.make_async_copy(frm, to, ad_sem.at[k])
        d.start()
        own_ads.append(d)
    theirs = pl.ds(pl.multiple_of((1 - c) * half, half), half)
    ours = pl.ds(pl.multiple_of(c * half, half), half)
    own_halves = []
    for mat, w in enumerate((gate, up)):
        d = pltpu.make_async_copy(w.at[:, ours], stage.at[mat, c], swap_own.at[mat])
        d.start()
        own_halves.append(d)

    barrier = pltpu.get_barrier_semaphore()
    peers = []
    for i in range(X):
        for j in range(A):
            for k in range(B):
                if i or j or k:
                    peers.append(moved(moved(moved(mine, "x", i), "a", j), "b", k))
    pl.semaphore_signal(barrier, inc=1, device_id=sib, device_id_type=MESH)
    for p in peers:
        pl.semaphore_signal(barrier, inc=1, device_id=p, device_id_type=MESH)
    count_req = chosen.shape[0]

    def look(s, got):
        here = stored[s]
        return tuple(jnp.where(here == chosen[r], s, g) for r, g in enumerate(got))

    found = lax.fori_loop(0, stored.shape[0], look, (jnp.int32(0),) * count_req)
    for r, s in enumerate(found):
        slot_of[r] = s
    for m in range(group_size):
        ask = jnp.int32(0)
        for s in found:
            ask = jnp.where(s // maps.shape[0] == m, s % maps.shape[0], ask)
        picks[m] = jnp.full(picks.shape[1:], ask, jnp.int32)

    pl.semaphore_wait(barrier, chips)

    sends = []
    swaps = []
    for mat, w in enumerate((gate, up)):
        s = pltpu.make_async_remote_copy(
            w.at[:, theirs], stage.at[mat, c], swap_send.at[mat], swap_recv.at[mat],
            device_id=sib, device_id_type=MESH,
        )
        s.start()
        swaps.append(s)

    for k, (frm, to) in enumerate(
        ((tokens, tok), (wk, wqkv.at[1]), (wq, wqkv.at[0]), (wv, wqkv.at[2]), (wo, wout))
    ):
        d = pltpu.make_async_copy(frm, to, load_sem.at[k])
        d.start()
        loads.append(d)

    def weight_slot(mat, span):
        start, width = spans[span]

        def get(chip):
            at = pl.ds(pl.multiple_of(chip * 2 * depth, 16), 2 * depth)
            return wide.at[mat, at, pl.ds(start, width)]

        return get

    items = []
    orders = ((("a", "x", "b"), ("a", "b", "x")), (("a", "x", "b"), ("b", "a", "x")),)
    weights = []
    for span in range(len(spans)):
        weights.append((len(items), len(items) + 1))
        for mat in range(2):
            items.append((weight_slot(mat, span), orders[span][mat]))

    line = (
        a,
        a + 1 - 2 * lax.rem(a, 2),
        jnp.where(a < A // 2, 2, 1),
        jnp.where(a < A // 2, A - 1, 0),
    )
    onward = tuple(2 * a - s if n == 1 else jnp.where(s < a, a + 1, a - 1) for n, s in enumerate(line))
    all_at = [
        {"x": i, "a": j, "b": k} for i in range(X) for j in range(A) for k in range(B)
    ]

    def place_of(rel):
        return {
            "x": lax.rem(x + rel["x"], X), "a": line[rel["a"]], "b": lax.rem(b + rel["b"], B)
        }

    def hops(rel):
        return rel["x"] + rel["a"] + rel["b"]

    count = [0]

    def push(n, chip, to, when):
        ref = items[n][0](chip)
        d = pltpu.make_async_remote_copy(
            ref, ref, i_send.at[count[0]], i_recv.at[n, chip], device_id=to, device_id_type=MESH
        )
        count[0] += 1
        sends.append((d, when))
        if when is None:
            d.start()
        else:
            pl.when(when)(d.start)

    def spread(n, rel):
        order = items[n][1]
        last = max([order.index(k) for k in order if rel[k]], default=-1)
        chip = chip_of(place_of(rel))
        for axis in order[max(last, 0):]:
            if axis == "a":
                if rel["a"] == 0:
                    push(n, chip, {"a": jnp.minimum(a + 1, A - 1)}, a + 1 < A)
                    push(n, chip, {"a": jnp.maximum(a - 1, 0)}, a > 0)
                else:
                    to = onward[rel["a"]]
                    push(n, chip, {"a": jnp.clip(to, 0, A - 1)}, (to >= 0) & (to < A))
            elif rel[axis] == 0:
                push(n, chip, {axis: 1 - mine[axis]}, None)

    def arrived(n, rel):
        chip = chip_of(place_of(rel))
        ref = items[n][0](chip)
        pltpu.make_async_remote_copy(
            ref, ref, i_send.at[0], i_recv.at[n, chip], device_id=sib, device_id_type=MESH
        ).wait_recv()

    def passes(n, rel):
        return hops(rel) > 0 and rel[items[n][1][2]] == 0

    def begin(ns):
        for n in ns:
            spread(n, all_at[0])

    def stage_of(ns, h):
        for n in ns:
            for rel in all_at:
                if hops(rel) == h and passes(n, rel):
                    arrived(n, rel)
                    spread(n, rel)

    def finish(ns):
        for n in ns:
            for rel in all_at:
                if hops(rel) and not passes(n, rel):
                    arrived(n, rel)

    partners = [(j, k) for j in range(A) for k in range(B) if j or k]

    def partner(n):
        return {"a": line[partners[n][0]], "b": lax.rem(b + partners[n][1], B)}

    def mp_of(at):
        return at["a"] * B + at["b"]

    for n in range(len(partners)):
        d = pltpu.make_async_remote_copy(
            picks.at[mp_of(partner(n))], asked.at[my_mp], q_send.at[n], q_recv.at[my_mp],
            device_id=partner(n), device_id_type=MESH,
        )
        d.start()
        sends.append((d, None))

    def chosen_map(asks):
        pick = asks[:1, :1]
        got = maps[0]
        for k in range(1, maps.shape[0]):
            got = jnp.where(pick == k, maps[k], got)
        return got

    def send_adapters():
        for d in own_ads:
            d.wait()
        for n in range(len(partners)):
            who = mp_of(partner(n))
            pltpu.make_async_remote_copy(
                picks.at[who], asked.at[who], q_send.at[n], q_recv.at[who],
                device_id=sib, device_id_type=MESH,
            ).wait_recv()
        for n in reversed(range(len(partners))):
            chosen_out[n] = chosen_map(asked[mp_of(partner(n))])
            d = pltpu.make_async_remote_copy(
                chosen_out.at[n], chosen_in.at[my_mp], m_send.at[n], m_recv.at[my_mp],
                device_id=partner(n), device_id_type=MESH,
            )
            d.start()
            sends.append((d, None))
        chosen_in[my_mp] = chosen_map(picks[my_mp])

    def adapters_here():
        for n in range(len(partners)):
            who = mp_of(partner(n))
            pltpu.make_async_remote_copy(
                chosen_out.at[n], chosen_in.at[who], m_send.at[n], m_recv.at[who],
                device_id=sib, device_id_type=MESH,
            ).wait_recv()

    def join_halves():
        for mat in range(2):
            own_halves[mat].wait()
            swaps[mat].wait()
            joined = jnp.concatenate(
                [stage[mat, 0].astype(f32), stage[mat, 1].astype(f32)], axis=0
            ).astype(bf16)
            wide[mat, pl.ds(pl.multiple_of(me * 2 * depth, 16), 2 * depth), :] = joined
    def norm_rows():
        loads[0].wait()

        @pl.loop(0, tok_dev, step=PAIR)
        def _(r):
            part = pl.ds(pl.multiple_of(r, PAIR), PAIR)
            wf = tok[part, :].astype(f32)
            scale = lax.rsqrt(jnp.mean(wf * wf, axis=-1, keepdims=True) + EPSILON)
            normed[part, :] = (wf * scale * gain1[...].reshape(1, span_embed)).astype(bf16)

    def project(k, to):
        loads[(2, 1, 3)[k]].wait()

        @pl.loop(0, tok_dev, step=256)
        def _(r):
            part = pl.ds(pl.multiple_of(r, 256), 256)
            to[part, :] = jnp.dot(
                normed[part, :], wqkv[k], preferred_element_type=f32
            ).astype(to.dtype)

    column = lax.broadcasted_iota(jnp.int32, (1, heads_wide), 1)

    def pair_step(pair, carry):
        for n in range(2):
            r = pair * 2 + n
            part = pl.ds(pl.multiple_of(r * SLOTR, SLOTR), SLOTR)
            owner = slot_of[r] // maps.shape[0]
            codes = lax.dot_general(
                normed[part, :], chosen_in[owner, :, :embed],
                (((1,), (1,)), ((), ())), preferred_element_type=f32,
            ).astype(bf16)
            g = chosen_in[owner, :, embed:]
            lane = lax.broadcasted_iota(jnp.int32, codes.shape, 1)
            none = jnp.zeros_like(codes)
            for low, base, to in ((True, qf, qb), (False, vf, vb)):
                kept = jnp.where((lane < LATENT_BREADTH) == low, codes, none)
                delta = jnp.dot(kept, g, preferred_element_type=f32) * PLUGIN_STRENGTH
                to[part, :] = (base[part, :] + delta.astype(bf16).astype(f32)).astype(bf16)
        part = pl.ds(pl.multiple_of(pair * PAIR, PAIR), PAIR)
        i = lax.broadcasted_iota(jnp.int32, (PAIR, PAIR), 0)
        j = lax.broadcasted_iota(jnp.int32, (PAIR, PAIR), 1)
        len0, len1 = lens[pair * 2], lens[pair * 2 + 1]
        qi = jnp.where(i < SLOTR, i, i - SLOTR)
        kj = jnp.where(j < SLOTR, j, j - SLOTR)
        same = (i < SLOTR) == (j < SLOTR)
        live = kj < jnp.where(j < SLOTR, len0, len1)
        seen = same & live & (kj <= qi) & ((qi - kj < WINDOW) | (kj < SINKS))
        row = lax.broadcasted_iota(jnp.int32, (PAIR, 1), 0)
        alive = jnp.where(row < SLOTR, row, row - SLOTR) < jnp.where(row < SLOTR, len0, len1)
        before = None
        for h in range(HEADS):
            lo, hi = h * HD, (h + 1) * HD
            first, last = lo // LANES, (hi - 1) // LANES
            cols = slice(first * LANES, (last + 1) * LANES)
            q = qb[part, cols]
            pick = (column[:, cols] >= lo) & (column[:, cols] < hi)
            q = jnp.where(pick, q, jnp.zeros_like(q))
            s = lax.dot_general(
                q, kb[part, cols], (((1,), (1,)), ((), ())), preferred_element_type=f32
            ) * HD ** (-0.5)
            s = jnp.where(seen, s, NEVER)
            e = jnp.where(seen, jnp.exp(s - jnp.max(s, axis=-1, keepdims=True)), 0.0)
            p = (e / jnp.sum(e, axis=-1, keepdims=True)).astype(bf16)
            o = jnp.dot(p, vb[part, cols], preferred_element_type=f32)
            o = jnp.where(alive, o, 0.0).astype(bf16)
            if h > 0:
                w = h - 1
                at = column[:, w * LANES:(w + 1) * LANES]
                att[part, w * LANES:(w + 1) * LANES] = jnp.where(at < lo, before, o[:, :LANES])
            before = o[:, -LANES:]
        return carry

    def attend_pairs(first, last):
        lax.fori_loop(first, last, pair_step, 0)

    group = source.shape[1]
    ahead = lax.broadcasted_iota(jnp.int32, (group, group), 0)
    turn = jnp.where(ahead == source[...], 1.0, 0.0).astype(bf16)

    def project_out():
        loads[4].wait()

        @pl.loop(0, tok_dev, step=PAIR)
        def _(r):
            part = pl.ds(pl.multiple_of(r, PAIR), PAIR)
            mixed = tok[part, :].astype(f32) + jnp.dot(
                att[part, :], wout[...], preferred_element_type=f32
            )
            mixed = mixed.astype(bf16)
            tok[part, :] = mixed
            wf = mixed.astype(f32)
            scale = lax.rsqrt(jnp.mean(wf * wf, axis=-1, keepdims=True) + EPSILON)
            nb = (wf * scale * gain2[...].reshape(1, span_embed)).astype(bf16)
            for g in range(span_embed // group):
                cols = slice(g * group, (g + 1) * group)
                act[part, cols] = jnp.dot(nb[:, cols], turn, preferred_element_type=f32).astype(bf16)

    res = pltpu.make_async_copy(tok, res_out, res_sem.at[0])
    own_rows = pltpu.make_async_copy(shuf.at[x, :, a, b], rows.at[:, x, c, a, b], r_recv.at[me])
    block = rows.shape[5]
    def regroup():
        res.start()
        size = A * B * block
        for i in range(X):
            for k in range(CORES):
                n = i * CORES + k
                rank = lax.broadcasted_iota(jnp.int32, (tok_dev, size), 0)
                one = jnp.where(rank == want[:, n * size:(n + 1) * size], 1.0, 0.0).astype(bf16)
                ordered = lax.dot_general(
                    one, act[...], (((0,), (0,)), ((), ())), preferred_element_type=f32
                ).astype(bf16)
                shuf[i, k] = ordered.reshape(A, B, block, span_embed)

        for k, p in enumerate(peers):
            d = pltpu.make_async_remote_copy(
                shuf.at[p["x"], :, p["a"], p["b"]], rows.at[:, x, c, a, b], r_send.at[k], r_recv.at[me],
                device_id=p, device_id_type=MESH,
            )
            d.start()
            sends.append((d, None))
        own_rows.start()

    def forward_rows(p, k):
        here = rows.at[:, p["x"], c, p["a"], p["b"]]
        d = pltpu.make_async_remote_copy(
            here, here, f_send.at[k], f_recv.at[k], device_id=sib, device_id_type=MESH
        )
        d.start()
        sends.append((d, None))

    def share_rows():
        own_rows.wait()
        forward_rows(mine, chips - 1)
        for k, p in enumerate(peers):
            here = rows.at[:, p["x"], c, p["a"], p["b"]]
            pltpu.make_async_remote_copy(
                here, here, r_send.at[k], r_recv.at[chip_of(p)], device_id=sib, device_id_type=MESH
            ).wait_recv()
            forward_rows(p, k)

    def rows_shared():
        for k, p in enumerate(peers + [mine]):
            here = rows.at[:, p["x"], 1 - c, p["a"], p["b"]]
            pltpu.make_async_remote_copy(
                here, here, f_send.at[k], f_recv.at[k], device_id=sib, device_id_type=MESH
            ).wait_recv()

    def result(strip, part):
        cols = pl.ds(pl.multiple_of(c * half + strip * STRIP, STRIP), STRIP)
        at = lax.rem(strip, 2)
        if part == 0:
            return pltpu.make_async_remote_copy(
                held.at[at, 0], hid_out.at[:, cols], o_send.at[at], o_recv.at[strip],
                device_id=sib, device_id_type=MESH,
            )
        return pltpu.make_async_copy(held.at[at, 1], hid_out.at[:, cols], o_own.at[at])

    def strip_step(strip, carry):
        @pl.when(strip >= 2)
        def _():
            result(strip - 2, 0).wait_send()
            result(strip - 2, 1).wait()

        cols = pl.ds(pl.multiple_of(strip * STRIP, STRIP), STRIP)
        for part in range(2):
            who = 1 - c if part == 0 else c
            mlp_in = rows[who].reshape(tok_dev, span_embed)
            g = jnp.dot(mlp_in, wide[0, :, cols], preferred_element_type=f32)
            u = jnp.dot(mlp_in, wide[1, :, cols], preferred_element_type=f32)
            held[lax.rem(strip, 2), part] = (g * jax.nn.sigmoid(g) * u).astype(bf16)
            result(strip, part).start()
        return carry

    def hidden_units(span):
        start, width = spans[span]
        finish(weights[span])
        lax.fori_loop(start // STRIP, (start + width) // STRIP, strip_step, 0)

    join_halves()
    begin(weights[1])
    begin(weights[0])
    send_adapters()
    norm_rows()
    stage_of(weights[1], 1)
    stage_of(weights[0], 1)
    project(1, kb)
    project(0, qf)
    stage_of(weights[1], 2)
    stage_of(weights[0], 2)
    project(2, vf)
    adapters_here()
    attend_pairs(0, 1)
    stage_of(weights[1], 3)
    attend_pairs(1, 3)
    stage_of(weights[0], 3)
    attend_pairs(3, 4)
    project_out()
    regroup()
    stage_of(weights[0], 4)
    stage_of(weights[1], 4)
    share_rows()
    rows_shared()
    hidden_units(0)
    hidden_units(1)
    strips = half // STRIP
    for s in (strips - 2, strips - 1):
        result(jnp.int32(s), 0).wait_send()
        result(jnp.int32(s), 1).wait()
    for s in range(strips):
        result(jnp.int32(s), 0).wait_recv()
    res.wait()
    for d, when in sends:
        if when is None:
            d.wait_send()
        else:
            pl.when(when)(d.wait_send)


def layer(shape, lens, chosen, stored, tokens, wq, wk, wv, wo, shrink, grow, gate, up, gain1, gain2, want, source):
    X, A, B = shape
    chips = X * A * B
    tok_dev, depth = tokens.shape
    heads_wide = wq.shape[1]
    shard, width = gate.shape
    half = width // CORES
    block = tok_dev // (chips * CORES)
    spans = ((0, 768), (768, half - 768))
    n_items = 2 * len(spans)
    resident, rank = shrink.shape[:2]
    DMA = pltpu.SemaphoreType.DMA
    bf16 = jnp.bfloat16
    f32 = jnp.float32
    ANY = pl.BlockSpec(memory_space=pl.ANY)
    VM = pl.BlockSpec(memory_space=pltpu.VMEM)
    SM = pl.BlockSpec(memory_space=pltpu.SMEM)
    return pl.pallas_call(
        functools.partial(layer_kernel, shape, spans),
        out_shape=(
            jax.ShapeDtypeStruct((tok_dev, depth), bf16),
            jax.ShapeDtypeStruct((tok_dev, width), bf16),
        ),
        in_specs=[SM] * 3 + [ANY] * 9 + [VM] * 4,
        out_specs=(ANY, ANY),
        scratch_shapes=[
            pltpu.VMEM((tok_dev, depth), bf16),
            pltpu.VMEM((3, depth, heads_wide), bf16),
            pltpu.VMEM((heads_wide, depth), bf16),
            pltpu.VMEM((tok_dev, depth), bf16),
            pltpu.VMEM((tok_dev, heads_wide), f32),
            pltpu.VMEM((tok_dev, heads_wide), f32),
            pltpu.VMEM((tok_dev, heads_wide), bf16),
            pltpu.VMEM((tok_dev, heads_wide), bf16),
            pltpu.VMEM((tok_dev, heads_wide), bf16),
            pltpu.VMEM((tok_dev, heads_wide), bf16),
            pltpu.VMEM((tok_dev, depth), bf16),
            pltpu.VMEM((X, CORES, A, B, block, depth), bf16),
            pltpu.SMEM((chosen.shape[0],), jnp.int32),
            pltpu.VMEM((resident, rank, depth + heads_wide), bf16),
            pltpu.VMEM((A * B, 8, LANES), jnp.int32),
            pltpu.VMEM((A * B, 8, LANES), jnp.int32),
            pltpu.VMEM((A * B - 1, rank, depth + heads_wide), bf16),
            pltpu.VMEM((A * B, rank, depth + heads_wide), bf16),
            pltpu.VMEM((2, CORES, shard, half), bf16),
            pltpu.VMEM((2, depth, half), bf16),
            pltpu.VMEM((CORES, X, CORES, A, B, block, depth), bf16),
            pltpu.VMEM((2, 2, tok_dev, STRIP), bf16),
            DMA((5,)), DMA((2,)), DMA((2,)), DMA((2,)), DMA((2,)),
            DMA((n_items * 2 * chips,)), DMA((n_items, chips)),
            DMA((A * B - 1,)), DMA((A * B,)), DMA((A * B - 1,)), DMA((A * B,)),
            DMA((chips,)), DMA((chips,)), DMA((chips,)), DMA((chips,)),
            DMA((2,)), DMA((2,)), DMA((half // STRIP,)), DMA((1,)),
        ],
        compiler_params=pltpu.CompilerParams(
            collective_id=0, has_side_effects=True, vmem_limit_bytes=62 << 20
        ),
        name="layer",
    )(lens, chosen, stored, tokens, wq, wk, wv, wo, shrink, grow, gate, up, gain1, gain2, want, source)


def local_fused(
    tokens, first_norm_gain, query_weight, key_weight, value_weight, output_weight, lengths,
    request_adapter, slot_adapter_ids, plugin_shrink_maps, plugin_grow_maps, device_token_order,
    second_norm_gain, gate_weight, up_weight,
):
    shape = tuple(lax.axis_size(n) for n in ("x", "a", "b"))
    mp = shape[1] * shape[2]
    resident = plugin_shrink_maps.shape[0]
    shard = gate_weight.shape[0]
    source = np.arange(CORES * mp * shard).reshape(CORES, mp, shard).transpose(1, 0, 2)
    return layer(
        shape, lengths, request_adapter, slot_adapter_ids, tokens, query_weight, key_weight, value_weight, output_weight,
        plugin_shrink_maps.transpose(0, 2, 1),
        plugin_grow_maps.reshape(resident, 2 * LATENT_BREADTH, -1),
        gate_weight, up_weight, first_norm_gain, second_norm_gain,
        device_token_order, jnp.asarray(source.reshape(1, -1), jnp.int32),
    )


def solution(mesh):
    dp, mp = mesh.devices.shape
    fast = 1
    while fast * fast * 4 <= mp:
        fast *= 2
    devices = dp * mp
    fits = (
        EMBED_SPAN // devices * CORES % 16 == 0
        and TOK_DEV // devices % 16 == 0
        and dp == APD
        and mp == 2 * APD
    )
    if fits:
        names = ("a", "b")
        fine = jax.sharding.Mesh(
            mesh.devices.reshape(dp // CORES, CORES, mp // fast, fast), ("x", "core", "a", "b")
        )
    else:
        names = ("mp",)
        fine = jax.sharding.Mesh(
            mesh.devices.reshape(dp // CORES, CORES, mp), ("x", "core", "mp")
        )
    rows = ("x", "core") + names
    return jax.shard_map(
        local_fused if fits else local_plain,
        mesh=fine,
        in_specs=(
            P(rows, None),
            P(),
            P(),
            P(),
            P(),
            P(),
            P(rows),
            P(rows),
            P(),
            P(names, None, None),
            P(names, None, None, None),
            P(rows, None),
            P(),
            P(rows, None),
            P(rows, None),
        ),
        out_specs=(P(rows, None), P(rows, None)),
        check_vma=False,
    )
```
